512 devices in a mesh: batch: 4 (over x_hi, core), space: 128 (over x_lo, y, z).
Axes of the slice: x: 4 (x_hi: 2, x_lo: 2; x = x_hi * 2 + x_lo), y: 8, z: 8, core: 2. Of those that a mesh axis runs over, the one named last changes fastest.
Arguments:
- inputs: bfloat16 [4, 32, 128, 128, 128], P('batch', None, None, 'space'), may hold values from -6 to 6
- pre_act: bfloat16 [4, 32, 128, 128, 128], P('batch', None, None, 'space'), may hold values from -8 to 8
- cotangent: bfloat16 [4, 32, 128, 128, 128], P('batch', None, None, 'space'), may hold values from -6 to 6
- spectral_weight: bfloat16 [2, 32, 32, 16384], P(None, None, None, 'space'), may hold values from -6 to 6
- skip_weight: bfloat16 [32, 32], replicated, may hold values from -1 to 1
Outputs:
- grad_inputs: bfloat16 [4, 32, 128, 128, 128], P('batch', None, None, 'space')
- grad_spectral: float32 [2, 32, 32, 16384], P(None, None, 'batch', 'space')
- grad_skip: float32 [32, 32], replicated
The draws below stay inside these ranges and needn't reach their ends.
All inputs are finite; a program needn't handle non-finite values.
Results may differ from the reference program's by a relative error of at most 0.0055.
Values sent between devices are 32-bit elements; how exact they have to be, the bound alone decides.
A program may use at most 64 MiB of HBM per device.

```python
import math
import jax
import jax.numpy as jnp
from jax import lax

NX = 128
NY = 128
NZ = 128
CHANNELS = 32
MX = 16
MY = 16
MZ = 16
BATCH = 4
MODES = 16384


def shard_levels(own_key, shape, shards, least, largest):
    def one(position, shards_of):
        steps = jax.random.uniform(jax.random.fold_in(jax.random.fold_in(own_key, 6), position), (shards_of,), jnp.float32, least / len(shards), largest / len(shards))
        return jnp.repeat(jnp.exp(steps), shape[position] // shards_of).reshape((-1,) + (1,) * (len(shape) - position - 1))

    gain = one(*shards[0])
    for cut in shards[1:]:
        gain = gain * one(*cut)
    return gain


def centred(stream_key, shape, deviation, most, pieces=(), kind=jnp.bfloat16):
    loudness = shard_levels(stream_key, shape, pieces, -0.22, 0.18) if pieces else 1.0
    entries = jax.random.normal(stream_key, shape, jnp.float32) * deviation * loudness
    return jnp.minimum(jnp.maximum(entries, -most), most).astype(kind)


def setup_inputs(seed: int = 0) -> dict:
    streams_of = jax.random.split(jax.random.key(seed), 6)
    return {
        "inputs": centred(streams_of[0], (BATCH, CHANNELS, NX, NY, NZ), 1.0, 6.0, ((0, 4), (3, 128))),
        "pre_act": centred(streams_of[1], (BATCH, CHANNELS, NX, NY, NZ), 1.5, 8.0, ((0, 4), (3, 128))),
        "cotangent": centred(streams_of[2], (BATCH, CHANNELS, NX, NY, NZ), 1.0, 6.0, ((0, 4), (3, 128))),
        "spectral_weight": centred(streams_of[3], (2, CHANNELS, CHANNELS, MODES), 1.0, 6.0, ((3, 128),)),
        "skip_weight": centred(streams_of[4], (CHANNELS, CHANNELS), CHANNELS ** -0.5, 1.0),
    }


HIGHEST = lax.Precision.HIGHEST

def phase_table(length, count, signed):
    points = jnp.arange(length, dtype=jnp.int32)
    orders = jnp.arange(count, dtype=jnp.int32)
    if signed:
        orders = jnp.where(orders < count // 2, orders, orders - count)
    residues = jnp.mod(points[:, None] * orders[None, :], length)
    radians = residues.astype(jnp.float32) * (2.0 * math.pi / length)
    return (jnp.cos(radians), jnp.sin(radians))

def forward_block(cosine, sine):
    return jnp.stack([jnp.stack([cosine, -sine], axis=1), jnp.stack([sine, cosine], axis=1)], axis=0)

def inverse_block(cosine, sine):
    cos_rows = cosine.T
    sin_rows = sine.T
    return jnp.stack([jnp.stack([cos_rows, sin_rows], axis=1), jnp.stack([-sin_rows, cos_rows], axis=1)], axis=0)

def gelu_slope(values):
    normal_cdf = 0.5 * (1.0 + jax.scipy.special.erf(values * (1.0 / math.sqrt(2.0))))
    density = jnp.exp(-0.5 * values * values) * (1.0 / math.sqrt(2.0 * math.pi))
    return normal_cdf + values * density

def to_float(values):
    return lax.optimization_barrier(values.astype(jnp.bfloat16)).astype(jnp.float32)

def spectrum(grid_in):
    cos_x, sin_x = phase_table(NX, 2 * MX, True)
    table_x = to_float(jnp.stack([cos_x, -sin_x], axis=1))
    section_x = jnp.einsum('cxyz,xpa->cpayz', grid_in.astype(jnp.float32), table_x, precision=HIGHEST)
    cos_z, sin_z = phase_table(NZ, MZ, False)
    section_z = jnp.einsum('cpayz,pzqk->cqyak', section_x, forward_block(cos_z, sin_z), precision=HIGHEST)
    section_z = section_z.reshape(CHANNELS, 2, NY, 2 * MX * MZ)
    cos_y, sin_y = phase_table(NY, 2 * MY, True)
    section_y = jnp.einsum('cpym,pyqk->cqmk', section_z, forward_block(cos_y, sin_y), precision=HIGHEST)
    return section_y.reshape(CHANNELS, 2, MODES)

def back_transform(spectra):
    cos_y, sin_y = phase_table(NY, 2 * MY, True)
    shaped = spectra.reshape(CHANNELS, 2, 2 * MX * MZ, 2 * MY)
    grid_y = jnp.einsum('cpmk,pkqy->cqym', shaped, inverse_block(cos_y, sin_y), precision=HIGHEST)
    grid_y = grid_y.reshape(CHANNELS, 2, NY, 2 * MX, MZ)
    cos_z, sin_z = phase_table(NZ, MZ, False)
    grid_z = jnp.einsum('cpyak,pkqz->cqayz', grid_y, inverse_block(cos_z, sin_z), precision=HIGHEST)
    cos_x, sin_x = phase_table(NX, 2 * MX, True)
    table_x = jnp.stack([cos_x.T, -sin_x.T], axis=0)
    return jnp.einsum('cpayz,pax->cxyz', grid_z, table_x, precision=HIGHEST)

def mode_scale():
    kz_index = jnp.arange(MODES, dtype=jnp.int32) // (2 * MY) % MZ
    return jnp.where(kz_index == 0, 1.0, 2.0).astype(jnp.float32) / float(NX * NY * NZ)

def cross_terms(spec_left, spec_right):
    real_part = jnp.einsum('im,om->iom', spec_left[:, 0], spec_right[:, 0], precision=HIGHEST)
    real_part = real_part + jnp.einsum('im,om->iom', spec_left[:, 1], spec_right[:, 1], precision=HIGHEST)
    imag_part = jnp.einsum('im,om->iom', spec_left[:, 0], spec_right[:, 1], precision=HIGHEST)
    imag_part = imag_part - jnp.einsum('im,om->iom', spec_left[:, 1], spec_right[:, 0], precision=HIGHEST)
    return jnp.stack([real_part, imag_part], axis=0)

def reference(inputs, pre_act, cotangent, spectral_weight, skip_weight):
    weights_full = spectral_weight.astype(jnp.float32)
    skip_full = skip_weight.astype(jnp.float32)
    scales = mode_scale()

    def one_sample(running, sample):
        grad_modes, grad_mix = running
        grid_in, pre_grid, cot_grid = sample
        cot_pre = (cot_grid.astype(jnp.float32) * gelu_slope(pre_grid.astype(jnp.float32))).astype(jnp.bfloat16)
        spec_u = spectrum(grid_in)
        spec_e = spectrum(cot_pre)
        grad_modes = grad_modes + cross_terms(spec_u, spec_e)
        rounded = to_float(spec_e)
        back_real = jnp.einsum('iom,om->im', weights_full[0], rounded[:, 0], precision=HIGHEST)
        back_real = back_real + jnp.einsum('iom,om->im', weights_full[1], rounded[:, 1], precision=HIGHEST)
        back_imag = jnp.einsum('iom,om->im', weights_full[0], rounded[:, 1], precision=HIGHEST)
        back_imag = back_imag - jnp.einsum('iom,om->im', weights_full[1], rounded[:, 0], precision=HIGHEST)
        back_modes = jnp.stack([back_real, back_imag], axis=1) * scales
        spatial = back_transform(back_modes)
        cot_full = cot_pre.astype(jnp.float32)
        mixed = jnp.einsum('io,oxyz->ixyz', skip_full, cot_full, precision=HIGHEST)
        grad_grid = (spatial + mixed).astype(jnp.bfloat16)
        grad_mix = grad_mix + jnp.einsum('ixyz,oxyz->io', grid_in.astype(jnp.float32), cot_full, precision=HIGHEST)
        return ((grad_modes, grad_mix), grad_grid)
    start_state = (jnp.zeros((2, CHANNELS, CHANNELS, MODES), jnp.float32), jnp.zeros((CHANNELS, CHANNELS), jnp.float32))
    (grad_modes, grad_mix), grad_inputs = lax.scan(one_sample, start_state, (inputs, pre_act, cotangent))
    grad_spectral = grad_modes * scales
    grad_skip = grad_mix / math.sqrt(BATCH * NX * NY * NZ)
    return (grad_inputs, grad_spectral, grad_skip)
```

```python
import math

import jax
import jax.numpy as jnp
import ml_dtypes
import numpy as np
from jax import lax
from jax.experimental import pallas as pl
from jax.experimental.pallas import tpu as pltpu
from jax.sharding import PartitionSpec as P

N = 128
MODES = 32
BATCH = 4
CHANNELS = 32
F32 = jnp.float32
BF16 = jnp.bfloat16
MESH = pl.DeviceIdType.MESH


def signed(index):
    return np.where(index < 16, index, index - 32)


def phases(points, orders):
    angles = np.mod(points[:, None] * orders[None, :], N) * (2.0 * math.pi / N)
    return np.cos(angles), np.sin(angles)


def bf16(table):
    return table.astype(np.float32).astype(ml_dtypes.bfloat16)


def places():
    t = np.arange(16)
    return t // 4, t // 2 % 2, t % 2


def make_tables():
    points = np.arange(N)
    eye = np.eye(8)
    cos_z, sin_z = (v.reshape(N, 4, 4) for v in phases(points, np.arange(16)))
    fwd_z = np.stack([np.einsum("zqk,cd->czqdk", v, eye) for v in (cos_z, -sin_z)], axis=2)
    fwd_z = fwd_z.reshape(8 * N, 256)
    inv_z = np.stack([np.einsum("zqk,cd->qckdz", v, eye) for v in (cos_z, -sin_z)], axis=0)
    inv_z = inv_z.reshape(256, 8 * N)
    cos_x, sin_x = phases(points, signed(np.arange(32)))
    cos_x, sin_x = bf16(cos_x).astype(np.float64), bf16(sin_x).astype(np.float64)
    parts = np.stack([np.stack([cos_x, sin_x]), np.stack([-sin_x, cos_x])])
    parts = parts.reshape(2, 2, N, 2, 8, 2)
    fwd_x = np.transpose(parts, (3, 5, 0, 4, 1, 2)).reshape(64, 256)
    cos_x, sin_x = phases(points, signed(np.arange(32)))
    parts = np.stack([np.stack([cos_x, -sin_x]), np.stack([sin_x, cos_x])]).reshape(2, 2, N, 2, 8, 2)
    inv_x = np.transpose(parts, (0, 2, 4, 3, 5, 1)).reshape(256, 64)
    q, a, h = places()
    y = a[None, :] * 64 + np.arange(8)[:, None] * 8 + h[None, :] * 4 + q[None, :]
    cos_y, sin_y = phases(y.reshape(-1), signed(np.arange(32)))
    cos_y, sin_y = cos_y.reshape(8, 16, 32), sin_y.reshape(8, 16, 32)
    parts = np.stack([np.stack([cos_y, sin_y]), np.stack([-sin_y, cos_y])])
    fwd_y = np.transpose(parts, (2, 3, 1, 0, 4))[:, :, :, :, None, :]
    fwd_y = np.broadcast_to(fwd_y, (8, 16, 2, 2, 4, 32)).reshape(256, 256)
    parts = np.stack([np.stack([cos_y, -sin_y]), np.stack([sin_y, cos_y])])
    inv_y = np.transpose(parts, (3, 0, 2, 1, 4))[:, :, :, :, None, :]
    inv_y = np.broadcast_to(inv_y, (16, 2, 8, 2, 4, 32)).reshape(256, 256)
    return tuple(bf16(v) for v in (fwd_z, fwd_x, fwd_y, inv_y, inv_x, inv_z))


def gelu_slope(values):
    normal_cdf = 0.5 * (1.0 + lax.erf(values * (1.0 / math.sqrt(2.0))))
    density = jnp.exp(-0.5 * values * values) * (1.0 / math.sqrt(2.0 * math.pi))
    return normal_cdf + values * density


def dot(left, right):
    return jnp.dot(left, right, preferred_element_type=F32)


def lanes(blocks):
    return jnp.concatenate(blocks, axis=1)


def to_modes(field, table_z, table_x, sent):
    sections = []
    for g in range(4):
        along_z = dot(lanes([field[8 * g + j] for j in range(8)]), table_z[...])
        both = jnp.concatenate([along_z[:, :N], along_z[:, N:]], axis=0).astype(BF16)
        sections.append(dot(table_x[...], both))
    for q in range(4):
        sent[64 * q : 64 * q + 64, :] = lanes([v[:, 32 * q : 32 * q + 32] for v in sections])


def turn(received, sent):
    for b in range(8):
        sent[b] = received[pl.ds(b, 32, stride=8), :]


def k4_lanes(rows):
    return lax.broadcasted_iota(jnp.int32, (rows, N), 1) // 32


def along_y(received, table_y, rows, put):
    both = lax.dot_general(
        received[...].reshape(256, N).astype(BF16),
        table_y[...],
        (((0,), (0,)), ((), ())),
        preferred_element_type=F32,
    )
    block = k4_lanes(32)
    for part in range(2):
        rows[part] = both[:, N * part : N * part + N]
        value = rows[part, pl.ds(0, 32, stride=4), :]
        for k4 in range(1, 4):
            value = jnp.where(block == k4, rows[part, pl.ds(k4, 32, stride=4), :], value)
        put(part, value)


def kernel(
    in_hbm, pre_hbm, cot_hbm, weight_hbm, skip_hbm,
    fz_hbm, fx_hbm, fy_hbm, iy_hbm, ix_hbm, iz_hbm,
    out_hbm, spectral_hbm, mixgrad_hbm,
    v_in, v_pre, v_cot, v_weight, v_skip, fz, fx, fy, iy, ix, iz,
    v_cp, v_mix, v_out, v_spectral, v_mixgrad,
    u_send, u_mid, u_turn, u_all, e_send, e_mid, e_turn, e_all, g_send, g_mid, g_turn, g_all,
    u_own, u_batch, e_own, e_batch, rows, partial, back_rows,
    prod, prod_rows, kron, skip_rows, m_own, m_one, m_two_own, m_two, m_three_own, m_three,
    load_sem, out_sem, send_sem, recv_sem,
):
    loads = [
        pltpu.make_async_copy(src, dst, load_sem.at[n])
        for n, (src, dst) in enumerate(
            (
                (in_hbm, v_in), (fz_hbm, fz), (fx_hbm, fx), (pre_hbm, v_pre), (cot_hbm, v_cot),
                (skip_hbm, v_skip), (fy_hbm, fy), (weight_hbm, v_weight), (iy_hbm, iy),
                (ix_hbm, ix), (iz_hbm, iz),
            )
        )
    ]
    for copy in loads:
        copy.start()

    sample = lax.axis_index("batch")
    place = lax.axis_index("space")
    a = place // 64
    b = place // 8 % 8
    h = place // 4 % 2
    q = place % 4
    t = 4 * q + 2 * a + h

    def near(k):
        peer = (t + k) % 16
        return peer, peer // 2 % 2 * 64 + b * 8 + peer % 2 * 4 + peer // 4

    def far(k):
        peer = (b + k) % 8
        return peer, a * 64 + peer * 8 + h * 4 + q

    def other(k):
        return (sample + k) % BATCH

    barrier = pltpu.get_barrier_semaphore()

    @pl.loop(1, 16)
    def _(k):
        pl.semaphore_signal(barrier, inc=1, device_id={"space": near(k)[1]}, device_id_type=MESH)

    @pl.loop(1, 8)
    def _(k):
        pl.semaphore_signal(barrier, inc=1, device_id={"space": far(k)[1]}, device_id_type=MESH)

    @pl.loop(1, BATCH)
    def _(k):
        pl.semaphore_signal(barrier, inc=1, device_id={"batch": other(k)}, device_id_type=MESH)

    def remote(src, dst, n, where):
        return pltpu.make_async_remote_copy(
            src_ref=src, dst_ref=dst, send_sem=send_sem.at[n], recv_sem=recv_sem.at[n],
            device_id=where, device_id_type=MESH,
        )

    def rows16(ref, slot):
        return ref.at[pl.ds(pl.multiple_of(slot * 16, 16), 16), :]

    def send_near(src, dst, n):
        pltpu.make_async_copy(rows16(src, t), rows16(dst, t), recv_sem.at[n]).start()

        @pl.loop(1, 16)
        def _(k):
            peer, where = near(k)
            remote(rows16(src, peer), rows16(dst, t), n, {"space": where}).start()

    def send_far(src, dst, n):
        pltpu.make_async_copy(src.at[b], dst.at[b], recv_sem.at[n]).start()

        @pl.loop(1, 8)
        def _(k):
            peer, where = far(k)
            remote(src.at[peer], dst.at[b], n, {"space": where}).start()

    def send_batch(src, dst, n):
        pltpu.make_async_copy(src, dst.at[sample], recv_sem.at[n]).start()

        @pl.loop(1, BATCH)
        def _(k):
            remote(src, dst.at[sample], n, {"batch": other(k)}).start()

    def arrived(ref, n):
        pltpu.make_async_copy(ref, ref, recv_sem.at[n]).wait()

    def left(ref, n):
        pltpu.make_async_copy(ref, ref, send_sem.at[n]).wait()

    for n in range(3):
        loads[n].wait()
    to_modes(v_in, fz, fx, u_send)
    pl.semaphore_wait(barrier, 15 + 7 + BATCH - 1)
    send_near(u_send, u_mid, 0)

    loads[3].wait()
    loads[4].wait()

    @pl.loop(0, CHANNELS)
    def _(c):
        slope = gelu_slope(v_pre[c].astype(F32))
        v_cp[c] = (v_cot[c].astype(F32) * slope).astype(BF16)

    to_modes(v_cp, fz, fx, e_send)
    send_near(e_send, e_mid, 1)
    arrived(u_mid, 0)
    turn(u_mid, u_turn)
    send_far(u_turn, u_all, 2)

    loads[5].wait()
    chunks = range(8)
    prod[...] = lax.dot_general(
        lanes([v_in[:, 16 * j : 16 * j + 16, :].reshape(512, N) for j in chunks]),
        lanes([v_cp[:, 16 * j : 16 * j + 16, :].reshape(512, N) for j in chunks]),
        (((1,), (1,)), ((), ())),
        preferred_element_type=F32,
    )
    row16 = lax.broadcasted_iota(jnp.int32, (16, 512), 0)
    column = lax.broadcasted_iota(jnp.int32, (16, 512), 1)
    same = row16 == column % 16
    for i in range(CHANNELS):
        kept = jnp.where(same, prod[16 * i : 16 * i + 16, :], 0.0)
        kept = kept[:8] + kept[8:]
        for n in range(4):
            prod_rows[n, 8 * i : 8 * i + 8, :] = kept[:, N * n : N * n + N]
    summed = []
    for n in range(4):
        value = prod_rows[n, pl.ds(0, 32, stride=8), :]
        for j in range(1, 8):
            value = value + prod_rows[n, pl.ds(j, 32, stride=8), :]
        summed.append(value)
    summed = lanes(summed)
    wide = lax.broadcasted_iota(jnp.int32, (512, 32), 0) // 16
    spread = wide == lax.broadcasted_iota(jnp.int32, (512, 32), 1)
    own = jnp.dot(
        summed, spread.astype(F32), precision=lax.Precision.HIGHEST, preferred_element_type=F32
    )
    m_own[...] = lanes([own[8 * r : 8 * r + 8, :] for r in range(4)])

    pltpu.make_async_copy(m_own, m_one.at[t], recv_sem.at[3]).start()

    @pl.loop(1, 16)
    def _(k):
        remote(m_own, m_one.at[t], 3, {"space": near(k)[1]}).start()

    arrived(e_mid, 1)
    turn(e_mid, e_turn)
    send_far(e_turn, e_all, 4)

    tall = lax.broadcasted_iota(jnp.int32, (32, 512), 1) // 16
    spread_t = tall == lax.broadcasted_iota(jnp.int32, (32, 512), 0)
    repeated = dot(v_skip[...], spread_t.astype(F32).astype(BF16))
    for n in range(4):
        skip_rows[n] = repeated[:, N * n : N * n + N]
    for i in range(CHANNELS):
        row = lanes([skip_rows[n, pl.ds(i, 16, stride=0), :] for n in range(4)])
        kron[16 * i : 16 * i + 16, :] = jnp.where(same, row, 0.0).astype(BF16)
    for j in range(0, 8, 2):
        pair = [v_cp[:, 16 * n : 16 * n + 16, :].reshape(512, N) for n in (j, j + 1)]
        mixed = dot(kron[...], lanes(pair))
        for n in range(2):
            v_mix[:, 16 * (j + n) : 16 * (j + n) + 16, :] = mixed[:, N * n : N * n + N].reshape(
                32, 16, N
            )

    arrived(u_all, 2)
    loads[6].wait()

    def put_u(part, value):
        u_own[32 * part : 32 * part + 32, :] = value

    along_y(u_all, fy, rows, put_u)
    send_batch(u_own, u_batch, 5)

    arrived(e_all, 4)
    e_rounded = []

    def put_e(part, value):
        for block in range(4):
            e_own[block, 8 * part : 8 * part + 8, :] = value[8 * block : 8 * block + 8, :]
        e_rounded.append(value.astype(BF16).astype(F32))

    along_y(e_all, fy, rows, put_e)

    loads[7].wait()
    e_real, e_imag = e_rounded
    for i in range(CHANNELS):
        w_real = v_weight[0, i].astype(F32)
        w_imag = v_weight[1, i].astype(F32)
        real = w_real * e_real + w_imag * e_imag
        imag = w_real * e_imag - w_imag * e_real
        for part, value in enumerate((real, imag)):
            partial[part, 8 * i : 8 * i + 8, :] = (
                value[0:8] + value[8:16] + (value[16:24] + value[24:32])
            )
    lane = lax.broadcasted_iota(jnp.int32, (1, N), 1)
    zero_kz = jnp.logical_and(q == 0, lane < 32)
    scale = jnp.where(zero_kz, 1.0, 2.0).astype(F32) / float(N * N * N)
    block = k4_lanes(32)
    for part in range(2):
        value = partial[part, pl.ds(0, 32, stride=8), :]
        for j in range(1, 8):
            value = value + partial[part, pl.ds(j, 32, stride=8), :]
        value = value * scale
        for k4 in range(4):
            back_rows[part, pl.ds(k4, 32, stride=4), :] = jnp.where(block == k4, value, 0.0)
    loads[8].wait()
    g_send[...] = lax.dot_general(
        iy[...],
        lanes([back_rows[0], back_rows[1]]).astype(BF16),
        (((1,), (1,)), ((), ())),
        preferred_element_type=F32,
    )
    send_near(g_send, g_mid, 6)

    pltpu.make_async_copy(e_own.at[sample], e_batch.at[sample], recv_sem.at[7]).start()

    @pl.loop(1, BATCH)
    def _(k):
        peer = other(k)
        remote(e_own.at[peer], e_batch.at[sample], 7, {"batch": peer}).start()

    arrived(m_one, 3)
    total = m_one[0]
    for n in range(1, 16):
        total = total + m_one[n]
    m_two_own[...] = total
    pltpu.make_async_copy(m_two_own, m_two.at[b], recv_sem.at[8]).start()

    @pl.loop(1, 8)
    def _(k):
        remote(m_two_own, m_two.at[b], 8, {"space": far(k)[1]}).start()

    arrived(g_mid, 6)
    turn(g_mid, g_turn)
    send_far(g_turn, g_all, 9)

    arrived(u_batch, 5)
    arrived(e_batch, 7)
    for i in range(CHANNELS):
        real = jnp.zeros((8, N), F32)
        imag = jnp.zeros((8, N), F32)
        for n in range(BATCH):
            u_real = u_batch[n, pl.ds(i, 8, stride=0), :]
            u_imag = u_batch[n, pl.ds(32 + i, 8, stride=0), :]
            e_r = e_batch[n, 0:8, :]
            e_i = e_batch[n, 8:16, :]
            real = real + (u_real * e_r + u_imag * e_i)
            imag = imag + (u_real * e_i - u_imag * e_r)
        v_spectral[0, i] = real * scale
        v_spectral[1, i] = imag * scale
    spectral_copy = pltpu.make_async_copy(v_spectral, spectral_hbm, out_sem.at[4])
    spectral_copy.start()

    arrived(m_two, 8)
    total = m_two[0]
    for n in range(1, 8):
        total = total + m_two[n]
    m_three_own[...] = total
    send_batch(m_three_own, m_three, 10)

    loads[9].wait()
    loads[10].wait()
    arrived(g_all, 9)
    outs = []
    for g in range(4):
        spectra = lanes(
            [
                g_all[:, 8 * n : 8 * n + 8, 32 * g : 32 * g + 32].reshape(64, 32)
                for n in range(4)
            ]
        )
        along_x = dot(ix[...], spectra.astype(BF16))
        both = lanes([along_x[:N], along_x[N:]]).astype(BF16)
        for n in range(4):
            grid = dot(both, iz[:, 256 * n : 256 * n + 256])
            for r in range(2):
                i = 8 * g + 2 * n + r
                v_out[i] = (grid[:, N * r : N * r + N] + v_mix[i]).astype(BF16)
        copy = pltpu.make_async_copy(
            v_out.at[8 * g : 8 * g + 8], out_hbm.at[8 * g : 8 * g + 8], out_sem.at[g]
        )
        copy.start()
        outs.append(copy)

    arrived(m_three, 10)
    total = (m_three[0] + m_three[1] + (m_three[2] + m_three[3])) / math.sqrt(BATCH * N * N * N)
    for r in range(4):
        v_mixgrad[8 * r : 8 * r + 8, :] = total[:, 32 * r : 32 * r + 32]
    mixgrad_copy = pltpu.make_async_copy(v_mixgrad, mixgrad_hbm, out_sem.at[5])
    mixgrad_copy.start()

    left(u_send.at[0:240], 0)
    left(e_send.at[0:240], 1)
    left(u_turn.at[0:7], 2)
    left(m_one.at[0:15], 3)
    left(e_turn.at[0:7], 4)
    left(u_batch.at[0:3], 5)
    left(g_send.at[0:240], 6)
    left(e_own.at[0:3], 7)
    left(m_two.at[0:7], 8)
    left(g_turn.at[0:7], 9)
    left(m_three.at[0:3], 10)
    for copy in outs:
        copy.wait()
    spectral_copy.wait()
    mixgrad_copy.wait()


def on_device(inputs, pre_act, cotangent, spectral_weight, skip_weight):
    field = (CHANNELS, N, N)
    tables = [jnp.asarray(v) for v in make_tables()]
    exchange = [
        pltpu.VMEM((256, N), F32), pltpu.VMEM((256, N), F32),
        pltpu.VMEM((8, 32, N), F32), pltpu.VMEM((8, 32, N), F32),
    ]
    anywhere = pl.BlockSpec(memory_space=pl.ANY)
    grad_inputs, grad_spectral, grad_skip = pl.pallas_call(
        kernel,
        out_shape=(
            jax.ShapeDtypeStruct(field, BF16),
            jax.ShapeDtypeStruct((2, CHANNELS, 8, N), F32),
            jax.ShapeDtypeStruct((CHANNELS, CHANNELS), F32),
        ),
        in_specs=[anywhere] * 11,
        out_specs=(anywhere,) * 3,
        scratch_shapes=[
            pltpu.VMEM(field, BF16), pltpu.VMEM(field, BF16), pltpu.VMEM(field, BF16),
            pltpu.VMEM((2, 32, 32, N), BF16), pltpu.VMEM((32, 32), BF16),
            *(pltpu.VMEM(v.shape, BF16) for v in tables),
            pltpu.VMEM(field, BF16), pltpu.VMEM(field, F32), pltpu.VMEM(field, BF16),
            pltpu.VMEM((2, 32, 8, N), F32), pltpu.VMEM((32, 32), F32),
            *exchange, *exchange, *exchange,
            pltpu.VMEM((64, N), F32), pltpu.VMEM((BATCH, 64, N), F32),
            pltpu.VMEM((4, 16, N), F32), pltpu.VMEM((BATCH, 16, N), F32),
            pltpu.VMEM((2, N, N), F32), pltpu.VMEM((2, 256, N), F32), pltpu.VMEM((2, N, N), F32),
            pltpu.VMEM((512, 512), F32), pltpu.VMEM((4, 256, N), F32),
            pltpu.VMEM((512, 512), BF16), pltpu.VMEM((4, 32, N), F32),
            pltpu.VMEM((8, N), F32), pltpu.VMEM((16, 8, N), F32),
            pltpu.VMEM((8, N), F32), pltpu.VMEM((8, 8, N), F32),
            pltpu.VMEM((8, N), F32), pltpu.VMEM((BATCH, 8, N), F32),
            pltpu.SemaphoreType.DMA((11,)), pltpu.SemaphoreType.DMA((6,)),
            pltpu.SemaphoreType.DMA((11,)), pltpu.SemaphoreType.DMA((11,)),
        ],
        compiler_params=pltpu.CompilerParams(
            collective_id=0, has_side_effects=True, vmem_limit_bytes=48 * 2**20
        ),
    )(
        inputs.reshape(field), pre_act.reshape(field), cotangent.reshape(field),
        spectral_weight, skip_weight, *tables,
    )
    return grad_inputs.reshape(inputs.shape), grad_spectral, grad_skip


def solution(mesh):
    placed = (
        P("batch", None, None, "space", None),
        P("batch", None, None, "space", None),
        P("batch", None, None, "space", None),
        P(None, None, None, "space"),
        P(),
    )
    return jax.shard_map(
        on_device,
        mesh=mesh,
        in_specs=placed,
        out_specs=(P("batch", None, None, "space", None), P(None, None, "batch", "space"), P()),
        check_vma=False,
    )
```

```python
import math

import jax
import jax.numpy as jnp
import ml_dtypes
import numpy as np
from jax import lax
from jax.experimental import pallas as pl
from jax.experimental.pallas import tpu as pltpu
from jax.sharding import PartitionSpec as P

N = 128
MODES = 32
BATCH = 4
CHANNELS = 32
F32 = jnp.float32
BF16 = jnp.bfloat16
MESH = pl.DeviceIdType.MESH


def signed(index):
    return np.where(index < 16, index, index - 32)


def phases(points, orders):
    angles = np.mod(points[:, None] * orders[None, :], N) * (2.0 * math.pi / N)
    return np.cos(angles), np.sin(angles)


def bf16(table):
    return table.astype(np.float32).astype(ml_dtypes.bfloat16)


def split(table):
    high = bf16(table)
    return high, bf16(table - high.astype(np.float64))


def places():
    t = np.arange(16)
    return t // 4, t // 2 % 2, t % 2


def make_tables():
    points = np.arange(N)
    eye = np.eye(8)
    cos_z, sin_z = (v.reshape(N, 4, 4) for v in phases(points, np.arange(16)))
    fwd_z = np.stack([np.einsum("zqk,cd->czqdk", v, eye) for v in (cos_z, -sin_z)], axis=2)
    fwd_z = fwd_z.reshape(8 * N, 256)
    inv_z = np.stack([np.einsum("zqk,cd->qckdz", v, eye) for v in (cos_z, -sin_z)], axis=0)
    inv_z = inv_z.reshape(256, 8 * N)
    cos_x, sin_x = phases(points, signed(np.arange(32)))
    cos_x, sin_x = bf16(cos_x).astype(np.float64), bf16(sin_x).astype(np.float64)
    parts = np.stack([np.stack([cos_x, sin_x]), np.stack([-sin_x, cos_x])])
    parts = parts.reshape(2, 2, N, 2, 8, 2)
    fwd_x = np.transpose(parts, (3, 5, 0, 4, 1, 2)).reshape(64, 256)
    cos_x, sin_x = phases(points, signed(np.arange(32)))
    parts = np.stack([np.stack([cos_x, -sin_x]), np.stack([sin_x, cos_x])]).reshape(2, 2, N, 2, 8, 2)
    inv_x = np.transpose(parts, (0, 2, 4, 3, 5, 1)).reshape(256, 64)
    q, a, h = places()
    y = a[None, :] * 64 + np.arange(8)[:, None] * 8 + h[None, :] * 4 + q[None, :]
    cos_y, sin_y = phases(y.reshape(-1), signed(np.arange(32)))
    cos_y, sin_y = cos_y.reshape(8, 16, 32), sin_y.reshape(8, 16, 32)
    parts = np.stack([np.stack([cos_y, sin_y]), np.stack([-sin_y, cos_y])])
    fwd_y = np.transpose(parts, (2, 3, 1, 0, 4))[:, :, :, :, None, :]
    fwd_y = np.broadcast_to(fwd_y, (8, 16, 2, 2, 4, 32)).reshape(256, 256)
    parts = np.stack([np.stack([cos_y, -sin_y]), np.stack([sin_y, cos_y])])
    inv_y = np.transpose(parts, (3, 0, 2, 1, 4))[:, :, :, :, None, :]
    inv_y = np.broadcast_to(inv_y, (16, 2, 8, 2, 4, 32)).reshape(256, 256)
    inv_x_high, inv_x_low = split(inv_x)
    inv_x = np.concatenate([inv_x_high, inv_x_high, inv_x_low], axis=1)
    fwd_y, inv_y = np.stack(split(fwd_y)), np.stack(split(inv_y))
    return bf16(fwd_z), bf16(fwd_x), fwd_y, inv_y, inv_x, bf16(inv_z)


def gelu_slope(values):
    normal_cdf = 0.5 * (1.0 + lax.erf(values * (1.0 / math.sqrt(2.0))))
    density = jnp.exp(-0.5 * values * values) * (1.0 / math.sqrt(2.0 * math.pi))
    return normal_cdf + values * density


def dot(left, right):
    return jnp.dot(left, right, preferred_element_type=F32)


def halves(value):
    high = value.astype(BF16)
    return high, (value - high.astype(F32)).astype(BF16)


def product(left, right, contracted):
    def one(first, second):
        return lax.dot_general(
            first, second, ((contracted[:1], contracted[1:]), ((), ())), preferred_element_type=F32
        )

    return one(left[0], right[0]) + (one(left[1], right[0]) + one(left[0], right[1]))


def lanes(blocks):
    return jnp.concatenate(blocks, axis=1)


def section(field, g, table_z, table_x):
    along_z = dot(lanes([field[8 * g + j] for j in range(8)]), table_z[...])
    both = jnp.concatenate([along_z[:, :N], along_z[:, N:]], axis=0).astype(BF16)
    return dot(table_x[...], both)


def to_blocks(sections, sent):
    for q in range(4):
        sent[64 * q : 64 * q + 64, :] = lanes([v[:, 32 * q : 32 * q + 32] for v in sections])


def turn(received, sent):
    for b in range(8):
        sent[b] = received[pl.ds(b, 32, stride=8), :]


def k4_lanes(rows):
    return lax.broadcasted_iota(jnp.int32, (rows, N), 1) // 32


def along_y(received, table_y, rows, put):
    both = product(
        halves(received[...].reshape(256, N)), (table_y[0], table_y[1]), (0, 0)
    )
    block = k4_lanes(32)
    for part in range(2):
        rows[part] = both[:, N * part : N * part + N]
        value = rows[part, pl.ds(0, 32, stride=4), :]
        for k4 in range(1, 4):
            value = jnp.where(block == k4, rows[part, pl.ds(k4, 32, stride=4), :], value)
        put(part, value)


def kernel(
    in_hbm, pre_hbm, cot_hbm, weight_hbm, skip_hbm,
    fz_hbm, fx_hbm, fy_hbm, iy_hbm, ix_hbm, iz_hbm,
    out_hbm, spectral_hbm, mixgrad_hbm,
    v_in, v_pre, v_cot, v_weight, v_skip, fz, fx, fy, iy, ix, iz,
    v_cp, v_mix, v_out, v_spectral, v_mixgrad,
    u_send, u_mid, u_turn, u_all, e_send, e_mid, e_turn, e_all, g_send, g_mid, g_turn, g_all,
    u_own, u_batch, e_own, e_batch, rows, partial, back_rows,
    prod, prod_rows, kron, skip_rows, m_own, m_one, m_two_own, m_two, m_three_own, m_three,
    load_sem, out_sem, send_sem, recv_sem,
):
    def group(ref, g):
        return ref.at[8 * g : 8 * g + 8]

    pairs = [(fz_hbm, fz)]
    for g in range(4):
        pairs += [(group(src, g), group(dst, g)) for src, dst in ((pre_hbm, v_pre), (cot_hbm, v_cot))]
    pairs += [
        (fx_hbm, fx), (in_hbm, v_in), (skip_hbm, v_skip), (fy_hbm, fy), (weight_hbm, v_weight),
        (iy_hbm, iy), (ix_hbm, ix), (iz_hbm, iz),
    ]
    loads = [
        pltpu.make_async_copy(src, dst, load_sem.at[n]) for n, (src, dst) in enumerate(pairs)
    ]
    for copy in loads:
        copy.start()

    sample = lax.axis_index("batch")
    place = lax.axis_index("space")
    a = place // 64
    b = place // 8 % 8
    h = place // 4 % 2
    q = place % 4
    t = 4 * q + 2 * a + h

    def near(k):
        peer = (t + k) % 16
        return peer, peer // 2 % 2 * 64 + b * 8 + peer % 2 * 4 + peer // 4

    def near_first():
        z = place % 8
        for step in (4, 3, 5, 2, 6, 1, 7, 0):
            c = (z + step) % 8
            for side in (1 - a, a):
                if step or side is not a:
                    yield c % 4 * 4 + side * 2 + c // 4, side * 64 + b * 8 + c

    def far(k):
        peer = (b + k) % 8
        return peer, a * 64 + peer * 8 + h * 4 + q

    def far_first():
        return [far(k) for k in (4, 3, 5, 2, 6, 1, 7)]

    def other(k):
        return (sample + k) % BATCH

    barrier = pltpu.get_barrier_semaphore()
    for _, where in [*near_first(), *far_first()]:
        pl.semaphore_signal(barrier, inc=1, device_id={"space": where}, device_id_type=MESH)

    @pl.loop(1, BATCH)
    def _(k):
        pl.semaphore_signal(barrier, inc=1, device_id={"batch": other(k)}, device_id_type=MESH)

    def remote(src, dst, n, where):
        return pltpu.make_async_remote_copy(
            src_ref=src, dst_ref=dst, send_sem=send_sem.at[n], recv_sem=recv_sem.at[n],
            device_id=where, device_id_type=MESH,
        )

    def rows16(ref, slot):
        return ref.at[pl.ds(pl.multiple_of(slot * 16, 16), 16), :]

    def send_near(src, dst, n):
        for peer, where in near_first():
            remote(rows16(src, peer), rows16(dst, t), n, {"space": where}).start()
        pltpu.make_async_copy(rows16(src, t), rows16(dst, t), recv_sem.at[n]).start()

    def send_far(src, dst, n):
        for peer, where in far_first():
            remote(src.at[peer], dst.at[b], n, {"space": where}).start()
        pltpu.make_async_copy(src.at[b], dst.at[b], recv_sem.at[n]).start()

    def send_batch(src, dst, n):
        pltpu.make_async_copy(src, dst.at[sample], recv_sem.at[n]).start()

        @pl.loop(1, BATCH)
        def _(k):
            remote(src, dst.at[sample], n, {"batch": other(k)}).start()

    def arrived(ref, n):
        pltpu.make_async_copy(ref, ref, recv_sem.at[n]).wait()

    def left(ref, n):
        pltpu.make_async_copy(ref, ref, send_sem.at[n]).wait()

    loads[0].wait()
    sections = []
    for g in range(4):
        loads[1 + 2 * g].wait()
        loads[2 + 2 * g].wait()
        for c in range(8 * g, 8 * g + 8):
            slope = gelu_slope(v_pre[c].astype(F32))
            v_cp[c] = (v_cot[c].astype(F32) * slope).astype(BF16)
        if g == 0:
            loads[9].wait()
        sections.append(section(v_cp, g, fz, fx))
    to_blocks(sections, e_send)
    pl.semaphore_wait(barrier, 15 + 7 + BATCH - 1)
    send_near(e_send, e_mid, 1)

    loads[10].wait()
    to_blocks([section(v_in, g, fz, fx) for g in range(4)], u_send)
    send_near(u_send, u_mid, 0)

    chunks = range(8)
    prod[...] = lax.dot_general(
        lanes([v_in[:, 16 * j : 16 * j + 16, :].reshape(512, N) for j in chunks]),
        lanes([v_cp[:, 16 * j : 16 * j + 16, :].reshape(512, N) for j in chunks]),
        (((1,), (1,)), ((), ())),
        preferred_element_type=F32,
    )
    row16 = lax.broadcasted_iota(jnp.int32, (16, 512), 0)
    column = lax.broadcasted_iota(jnp.int32, (16, 512), 1)
    same = row16 == column % 16
    for i in range(CHANNELS):
        kept = jnp.where(same, prod[16 * i : 16 * i + 16, :], 0.0)
        kept = kept[:8] + kept[8:]
        for n in range(4):
            prod_rows[n, 8 * i : 8 * i + 8, :] = kept[:, N * n : N * n + N]
    summed = []
    for n in range(4):
        value = prod_rows[n, pl.ds(0, 32, stride=8), :]
        for j in range(1, 8):
            value = value + prod_rows[n, pl.ds(j, 32, stride=8), :]
        summed.append(value)
    summed = lanes(summed)
    wide = lax.broadcasted_iota(jnp.int32, (512, 32), 0) // 16
    spread = wide == lax.broadcasted_iota(jnp.int32, (512, 32), 1)
    own = jnp.dot(
        summed, spread.astype(F32), precision=lax.Precision.HIGHEST, preferred_element_type=F32
    )
    m_own[...] = lanes([own[8 * r : 8 * r + 8, :] for r in range(4)])

    pltpu.make_async_copy(m_own, m_one.at[t], recv_sem.at[3]).start()

    @pl.loop(1, 16)
    def _(k):
        remote(m_own, m_one.at[t], 3, {"space": near(k)[1]}).start()

    arrived(e_mid, 1)
    turn(e_mid, e_turn)
    send_far(e_turn, e_all, 4)
    arrived(u_mid, 0)
    turn(u_mid, u_turn)
    send_far(u_turn, u_all, 2)

    loads[11].wait()
    tall = lax.broadcasted_iota(jnp.int32, (32, 512), 1) // 16
    spread_t = tall == lax.broadcasted_iota(jnp.int32, (32, 512), 0)
    repeated = dot(v_skip[...], spread_t.astype(F32).astype(BF16))
    for n in range(4):
        skip_rows[n] = repeated[:, N * n : N * n + N]
    for i in range(CHANNELS):
        row = lanes([skip_rows[n, pl.ds(i, 16, stride=0), :] for n in range(4)])
        kron[16 * i : 16 * i + 16, :] = jnp.where(same, row, 0.0).astype(BF16)
    for j in range(0, 8, 2):
        pair = [v_cp[:, 16 * n : 16 * n + 16, :].reshape(512, N) for n in (j, j + 1)]
        mixed = dot(kron[...], lanes(pair))
        for n in range(2):
            v_mix[:, 16 * (j + n) : 16 * (j + n) + 16, :] = mixed[:, N * n : N * n + N].reshape(
                32, 16, N
            )

    arrived(e_all, 4)
    loads[12].wait()
    e_rounded = []

    def put_e(part, value):
        for block in range(4):
            e_own[block, 8 * part : 8 * part + 8, :] = value[8 * block : 8 * block + 8, :]
        e_rounded.append(value.astype(BF16).astype(F32))

    along_y(e_all, fy, rows, put_e)

    loads[13].wait()
    e_real, e_imag = e_rounded
    for i in range(CHANNELS):
        w_real = v_weight[0, i].astype(F32)
        w_imag = v_weight[1, i].astype(F32)
        real = w_real * e_real + w_imag * e_imag
        imag = w_real * e_imag - w_imag * e_real
        for part, value in enumerate((real, imag)):
            partial[part, 8 * i : 8 * i + 8, :] = (
                value[0:8] + value[8:16] + (value[16:24] + value[24:32])
            )
    lane = lax.broadcasted_iota(jnp.int32, (1, N), 1)
    zero_kz = jnp.logical_and(q == 0, lane < 32)
    scale = jnp.where(zero_kz, 1.0, 2.0).astype(F32) / float(N * N * N)
    block = k4_lanes(32)
    for part in range(2):
        value = partial[part, pl.ds(0, 32, stride=8), :]
        for j in range(1, 8):
            value = value + partial[part, pl.ds(j, 32, stride=8), :]
        value = value * scale
        for k4 in range(4):
            back_rows[part, pl.ds(k4, 32, stride=4), :] = jnp.where(block == k4, value, 0.0)
    loads[14].wait()
    back = halves(lanes([back_rows[0], back_rows[1]]))
    g_send[...] = product((iy[0], iy[1]), back, (1, 1))
    send_near(g_send, g_mid, 6)

    pltpu.make_async_copy(e_own.at[sample], e_batch.at[sample], recv_sem.at[7]).start()

    @pl.loop(1, BATCH)
    def _(k):
        peer = other(k)
        remote(e_own.at[peer], e_batch.at[sample], 7, {"batch": peer}).start()

    arrived(u_all, 2)

    def put_u(part, value):
        u_own[32 * part : 32 * part + 32, :] = value

    along_y(u_all, fy, rows, put_u)
    send_batch(u_own, u_batch, 5)

    arrived(m_one, 3)
    total = m_one[0]
    for n in range(1, 16):
        total = total + m_one[n]
    m_two_own[...] = total
    pltpu.make_async_copy(m_two_own, m_two.at[b], recv_sem.at[8]).start()

    @pl.loop(1, 8)
    def _(k):
        remote(m_two_own, m_two.at[b], 8, {"space": far(k)[1]}).start()

    arrived(g_mid, 6)
    turn(g_mid, g_turn)
    send_far(g_turn, g_all, 9)

    arrived(u_batch, 5)
    arrived(e_batch, 7)
    for i in range(CHANNELS):
        real = jnp.zeros((8, N), F32)
        imag = jnp.zeros((8, N), F32)
        for n in range(BATCH):
            u_real = u_batch[n, pl.ds(i, 8, stride=0), :]
            u_imag = u_batch[n, pl.ds(32 + i, 8, stride=0), :]
            e_r = e_batch[n, 0:8, :]
            e_i = e_batch[n, 8:16, :]
            real = real + (u_real * e_r + u_imag * e_i)
            imag = imag + (u_real * e_i - u_imag * e_r)
        v_spectral[0, i] = real * scale
        v_spectral[1, i] = imag * scale
    spectral_copy = pltpu.make_async_copy(v_spectral, spectral_hbm, out_sem.at[4])
    spectral_copy.start()

    arrived(m_two, 8)
    total = m_two[0]
    for n in range(1, 8):
        total = total + m_two[n]
    m_three_own[...] = total
    send_batch(m_three_own, m_three, 10)

    loads[15].wait()
    loads[16].wait()
    arrived(g_all, 9)
    outs = []
    for g in range(4):
        spectra = lanes(
            [
                g_all[:, 8 * n : 8 * n + 8, 32 * g : 32 * g + 32].reshape(64, 32)
                for n in range(4)
            ]
        )
        high, low = halves(spectra)
        along_x = dot(ix[...], jnp.concatenate([high, low, high], axis=0))
        both = lanes([along_x[:N], along_x[N:]]).astype(BF16)
        for n in range(4):
            grid = dot(both, iz[:, 256 * n : 256 * n + 256])
            for r in range(2):
                i = 8 * g + 2 * n + r
                v_out[i] = (grid[:, N * r : N * r + N] + v_mix[i]).astype(BF16)
        copy = pltpu.make_async_copy(
            v_out.at[8 * g : 8 * g + 8], out_hbm.at[8 * g : 8 * g + 8], out_sem.at[g]
        )
        copy.start()
        outs.append(copy)

    arrived(m_three, 10)
    total = (m_three[0] + m_three[1] + (m_three[2] + m_three[3])) / math.sqrt(BATCH * N * N * N)
    for r in range(4):
        v_mixgrad[8 * r : 8 * r + 8, :] = total[:, 32 * r : 32 * r + 32]
    mixgrad_copy = pltpu.make_async_copy(v_mixgrad, mixgrad_hbm, out_sem.at[5])
    mixgrad_copy.start()

    left(u_send.at[0:240], 0)
    left(e_send.at[0:240], 1)
    left(u_turn.at[0:7], 2)
    left(m_one.at[0:15], 3)
    left(e_turn.at[0:7], 4)
    left(u_batch.at[0:3], 5)
    left(g_send.at[0:240], 6)
    left(e_own.at[0:3], 7)
    left(m_two.at[0:7], 8)
    left(g_turn.at[0:7], 9)
    left(m_three.at[0:3], 10)
    for copy in outs:
        copy.wait()
    spectral_copy.wait()
    mixgrad_copy.wait()


def on_device(inputs, pre_act, cotangent, spectral_weight, skip_weight):
    field = (CHANNELS, N, N)
    tables = [jnp.asarray(v) for v in make_tables()]
    exchange = [
        pltpu.VMEM((256, N), F32), pltpu.VMEM((256, N), F32),
        pltpu.VMEM((8, 32, N), F32), pltpu.VMEM((8, 32, N), F32),
    ]
    anywhere = pl.BlockSpec(memory_space=pl.ANY)
    grad_inputs, grad_spectral, grad_skip = pl.pallas_call(
        kernel,
        out_shape=(
            jax.ShapeDtypeStruct(field, BF16),
            jax.ShapeDtypeStruct((2, CHANNELS, 8, N), F32),
            jax.ShapeDtypeStruct((CHANNELS, CHANNELS), F32),
        ),
        in_specs=[anywhere] * 11,
        out_specs=(anywhere,) * 3,
        scratch_shapes=[
            pltpu.VMEM(field, BF16), pltpu.VMEM(field, BF16), pltpu.VMEM(field, BF16),
            pltpu.VMEM((2, 32, 32, N), BF16), pltpu.VMEM((32, 32), BF16),
            *(pltpu.VMEM(v.shape, BF16) for v in tables),
            pltpu.VMEM(field, BF16), pltpu.VMEM(field, F32), pltpu.VMEM(field, BF16),
            pltpu.VMEM((2, 32, 8, N), F32), pltpu.VMEM((32, 32), F32),
            *exchange, *exchange, *exchange,
            pltpu.VMEM((64, N), F32), pltpu.VMEM((BATCH, 64, N), F32),
            pltpu.VMEM((4, 16, N), F32), pltpu.VMEM((BATCH, 16, N), F32),
            pltpu.VMEM((2, N, N), F32), pltpu.VMEM((2, 256, N), F32), pltpu.VMEM((2, N, N), F32),
            pltpu.VMEM((512, 512), F32), pltpu.VMEM((4, 256, N), F32),
            pltpu.VMEM((512, 512), BF16), pltpu.VMEM((4, 32, N), F32),
            pltpu.VMEM((8, N), F32), pltpu.VMEM((16, 8, N), F32),
            pltpu.VMEM((8, N), F32), pltpu.VMEM((8, 8, N), F32),
            pltpu.VMEM((8, N), F32), pltpu.VMEM((BATCH, 8, N), F32),
            pltpu.SemaphoreType.DMA((17,)), pltpu.SemaphoreType.DMA((6,)),
            pltpu.SemaphoreType.DMA((11,)), pltpu.SemaphoreType.DMA((11,)),
        ],
        compiler_params=pltpu.CompilerParams(
            collective_id=0, has_side_effects=True, vmem_limit_bytes=62 * 2**20
        ),
    )(
        inputs.reshape(field), pre_act.reshape(field), cotangent.reshape(field),
        spectral_weight, skip_weight, *tables,
    )
    return grad_inputs.reshape(inputs.shape), grad_spectral, grad_skip


def solution(mesh):
    placed = (
        P("batch", None, None, "space", None),
        P("batch", None, None, "space", None),
        P("batch", None, None, "space", None),
        P(None, None, None, "space"),
        P(),
    )
    return jax.shard_map(
        on_device,
        mesh=mesh,
        in_specs=placed,
        out_specs=(P("batch", None, None, "space", None), P(None, None, "batch", "space"), P()),
        check_vma=False,
    )
```

```python
import math

import jax
import jax.numpy as jnp
import ml_dtypes
import numpy as np
from jax import lax
from jax.experimental import pallas as pl
from jax.experimental.pallas import tpu as pltpu
from jax.sharding import PartitionSpec as P

N = 128
MODES = 32
BATCH = 4
CHANNELS = 32
F32 = jnp.float32
BF16 = jnp.bfloat16
MESH = pl.DeviceIdType.MESH


def signed(index):
    return np.where(index < 16, index, index - 32)


def phases(points, orders):
    angles = np.mod(points[:, None] * orders[None, :], N) * (2.0 * math.pi / N)
    return np.cos(angles), np.sin(angles)


def bf16(table):
    return table.astype(np.float32).astype(ml_dtypes.bfloat16)


def split(table):
    high = bf16(table)
    return high, bf16(table - high.astype(np.float64))


def places():
    t = np.arange(16)
    return t // 4, t // 2 % 2, t % 2


def make_tables():
    points = np.arange(N)
    eye = np.eye(8)
    cos_z, sin_z = (v.reshape(N, 4, 4) for v in phases(points, np.arange(16)))
    fwd_z = np.stack([np.einsum("zqk,cd->czqdk", v, eye) for v in (cos_z, -sin_z)], axis=2)
    fwd_z = fwd_z.reshape(8 * N, 256)
    inv_z = np.stack([np.einsum("zqk,cd->qckdz", v, eye) for v in (cos_z, -sin_z)], axis=0)
    inv_z = inv_z.reshape(256, 8 * N)
    cos_x, sin_x = phases(points, signed(np.arange(32)))
    cos_x, sin_x = bf16(cos_x).astype(np.float64), bf16(sin_x).astype(np.float64)
    parts = np.stack([np.stack([cos_x, sin_x]), np.stack([-sin_x, cos_x])])
    parts = parts.reshape(2, 2, N, 2, 8, 2)
    fwd_x = np.transpose(parts, (3, 5, 0, 4, 1, 2)).reshape(64, 256)
    cos_x, sin_x = phases(points, signed(np.arange(32)))
    parts = np.stack([np.stack([cos_x, -sin_x]), np.stack([sin_x, cos_x])]).reshape(2, 2, N, 2, 8, 2)
    inv_x = np.transpose(parts, (0, 2, 4, 3, 5, 1)).reshape(256, 64)
    q, a, h = places()
    y = a[None, :] * 64 + np.arange(8)[:, None] * 8 + h[None, :] * 4 + q[None, :]
    cos_y, sin_y = phases(y.reshape(-1), signed(np.arange(32)))
    cos_y, sin_y = cos_y.reshape(8, 16, 32), sin_y.reshape(8, 16, 32)
    parts = np.stack([np.stack([cos_y, sin_y]), np.stack([-sin_y, cos_y])])
    fwd_y = np.transpose(parts, (2, 3, 1, 0, 4))[:, :, :, :, None, :]
    fwd_y = np.broadcast_to(fwd_y, (8, 16, 2, 2, 4, 32)).reshape(256, 256)
    parts = np.stack([np.stack([cos_y, -sin_y]), np.stack([sin_y, cos_y])])
    inv_y = np.transpose(parts, (3, 0, 2, 1, 4))[:, :, :, :, None, :]
    inv_y = np.broadcast_to(inv_y, (16, 2, 8, 2, 4, 32)).reshape(256, 256)
    inv_x_high, inv_x_low = split(inv_x)
    inv_x = np.concatenate([inv_x_high, inv_x_high, inv_x_low], axis=1)
    fwd_y, inv_y = np.stack(split(fwd_y)), np.stack(split(inv_y))
    return bf16(fwd_z), bf16(fwd_x), fwd_y, inv_y, inv_x, bf16(inv_z)


def gelu_slope(values):
    normal_cdf = 0.5 * (1.0 + lax.erf(values * (1.0 / math.sqrt(2.0))))
    density = jnp.exp(-0.5 * values * values) * (1.0 / math.sqrt(2.0 * math.pi))
    return normal_cdf + values * density


def dot(left, right):
    return jnp.dot(left, right, preferred_element_type=F32)


def halves(value):
    high = value.astype(BF16)
    return high, (value - high.astype(F32)).astype(BF16)


def product(left, right, contracted):
    def one(first, second):
        return lax.dot_general(
            first, second, ((contracted[:1], contracted[1:]), ((), ())), preferred_element_type=F32
        )

    return one(left[0], right[0]) + (one(left[1], right[0]) + one(left[0], right[1]))


def lanes(blocks):
    return jnp.concatenate(blocks, axis=1)


def section(field, g, table_z, table_x):
    along_z = dot(lanes([field[8 * g + j] for j in range(8)]), table_z[...])
    both = jnp.concatenate([along_z[:, :N], along_z[:, N:]], axis=0).astype(BF16)
    return dot(table_x[...], both)


def to_blocks(sections, sent):
    for q in range(4):
        sent[64 * q : 64 * q + 64, :] = lanes([v[:, 32 * q : 32 * q + 32] for v in sections])


def turn(received, sent):
    for b in range(8):
        sent[b] = received[pl.ds(b, 32, stride=8), :]


def k4_lanes(rows):
    return lax.broadcasted_iota(jnp.int32, (rows, N), 1) // 32


def along_y(received, table_y, rows, put):
    both = product(
        halves(received[...].reshape(256, N)), (table_y[0], table_y[1]), (0, 0)
    )
    block = k4_lanes(32)
    for part in range(2):
        rows[part] = both[:, N * part : N * part + N]
        value = rows[part, pl.ds(0, 32, stride=4), :]
        for k4 in range(1, 4):
            value = jnp.where(block == k4, rows[part, pl.ds(k4, 32, stride=4), :], value)
        put(part, value)


def spectral_kernel(
    in_hbm, pre_hbm, cot_hbm, weight_hbm, skip_hbm,
    fz_hbm, fx_hbm, fy_hbm, iy_hbm, ix_hbm, iz_hbm,
    v_grid, v_mix, ix, iz, v_spectral, v_mixgrad,
    v_in, v_pre, v_cot, v_weight, v_skip, fz, fx, fy, iy,
    v_cp,
    u_send, u_mid, u_turn, u_all, e_send, e_mid, e_turn, e_all, g_send, g_mid, g_turn, g_all,
    u_own, u_batch, e_own, e_batch, rows, partial, back_rows,
    prod, prod_rows, kron, skip_rows, m_own, m_one, m_two_own, m_two, m_three_own, m_three,
    load_sem, send_sem, recv_sem,
):
    def group(ref, g):
        return ref.at[8 * g : 8 * g + 8]

    pairs = [(fz_hbm, fz)]
    for g in range(4):
        pairs += [(group(src, g), group(dst, g)) for src, dst in ((pre_hbm, v_pre), (cot_hbm, v_cot))]
    pairs += [
        (fx_hbm, fx), (in_hbm, v_in), (skip_hbm, v_skip), (fy_hbm, fy), (weight_hbm, v_weight),
        (iy_hbm, iy), (ix_hbm, ix), (iz_hbm, iz),
    ]
    loads = [
        pltpu.make_async_copy(src, dst, load_sem.at[n]) for n, (src, dst) in enumerate(pairs)
    ]
    for copy in loads:
        copy.start()

    sample = lax.axis_index("batch")
    place = lax.axis_index("space")
    a = place // 64
    b = place // 8 % 8
    h = place // 4 % 2
    q = place % 4
    t = 4 * q + 2 * a + h

    def near(k):
        peer = (t + k) % 16
        return peer, peer // 2 % 2 * 64 + b * 8 + peer % 2 * 4 + peer // 4

    def near_first():
        z = place % 8
        for step in (4, 3, 5, 2, 6, 1, 7, 0):
            c = (z + step) % 8
            for side in (1 - a, a):
                if step or side is not a:
                    yield c % 4 * 4 + side * 2 + c // 4, side * 64 + b * 8 + c

    def far(k):
        peer = (b + k) % 8
        return peer, a * 64 + peer * 8 + h * 4 + q

    def far_first():
        return [far(k) for k in (4, 3, 5, 2, 6, 1, 7)]

    def other(k):
        return (sample + k) % BATCH

    barrier = pltpu.get_barrier_semaphore()
    for _, where in [*near_first(), *far_first()]:
        pl.semaphore_signal(barrier, inc=1, device_id={"space": where}, device_id_type=MESH)

    @pl.loop(1, BATCH)
    def _(k):
        pl.semaphore_signal(barrier, inc=1, device_id={"batch": other(k)}, device_id_type=MESH)

    def remote(src, dst, n, where):
        return pltpu.make_async_remote_copy(
            src_ref=src, dst_ref=dst, send_sem=send_sem.at[n], recv_sem=recv_sem.at[n],
            device_id=where, device_id_type=MESH,
        )

    def rows16(ref, slot):
        return ref.at[pl.ds(pl.multiple_of(slot * 16, 16), 16), :]

    def send_near(src, dst, n):
        for peer, where in near_first():
            remote(rows16(src, peer), rows16(dst, t), n, {"space": where}).start()
        pltpu.make_async_copy(rows16(src, t), rows16(dst, t), recv_sem.at[n]).start()

    def send_far(src, dst, n):
        for peer, where in far_first():
            remote(src.at[peer], dst.at[b], n, {"space": where}).start()
        pltpu.make_async_copy(src.at[b], dst.at[b], recv_sem.at[n]).start()

    def send_batch(src, dst, n):
        pltpu.make_async_copy(src, dst.at[sample], recv_sem.at[n]).start()

        @pl.loop(1, BATCH)
        def _(k):
            remote(src, dst.at[sample], n, {"batch": other(k)}).start()

    def arrived(ref, n):
        pltpu.make_async_copy(ref, ref, recv_sem.at[n]).wait()

    def left(ref, n):
        pltpu.make_async_copy(ref, ref, send_sem.at[n]).wait()

    loads[0].wait()
    sections = []
    for g in range(4):
        loads[1 + 2 * g].wait()
        loads[2 + 2 * g].wait()
        for c in range(8 * g, 8 * g + 8):
            slope = gelu_slope(v_pre[c].astype(F32))
            v_cp[c] = (v_cot[c].astype(F32) * slope).astype(BF16)
        if g == 0:
            loads[9].wait()
        sections.append(section(v_cp, g, fz, fx))
    to_blocks(sections, e_send)
    pl.semaphore_wait(barrier, 15 + 7 + BATCH - 1)
    send_near(e_send, e_mid, 1)

    loads[10].wait()
    to_blocks([section(v_in, g, fz, fx) for g in range(4)], u_send)
    send_near(u_send, u_mid, 0)

    chunks = range(8)
    prod[...] = lax.dot_general(
        lanes([v_in[:, 16 * j : 16 * j + 16, :].reshape(512, N) for j in chunks]),
        lanes([v_cp[:, 16 * j : 16 * j + 16, :].reshape(512, N) for j in chunks]),
        (((1,), (1,)), ((), ())),
        preferred_element_type=F32,
    )
    row16 = lax.broadcasted_iota(jnp.int32, (16, 512), 0)
    column = lax.broadcasted_iota(jnp.int32, (16, 512), 1)
    same = row16 == column % 16
    for i in range(CHANNELS):
        kept = jnp.where(same, prod[16 * i : 16 * i + 16, :], 0.0)
        kept = kept[:8] + kept[8:]
        for n in range(4):
            prod_rows[n, 8 * i : 8 * i + 8, :] = kept[:, N * n : N * n + N]
    summed = []
    for n in range(4):
        value = prod_rows[n, pl.ds(0, 32, stride=8), :]
        for j in range(1, 8):
            value = value + prod_rows[n, pl.ds(j, 32, stride=8), :]
        summed.append(value)
    summed = lanes(summed)
    wide = lax.broadcasted_iota(jnp.int32, (512, 32), 0) // 16
    spread = wide == lax.broadcasted_iota(jnp.int32, (512, 32), 1)
    own = jnp.dot(
        summed, spread.astype(F32), precision=lax.Precision.HIGHEST, preferred_element_type=F32
    )
    m_own[...] = lanes([own[8 * r : 8 * r + 8, :] for r in range(4)])

    pltpu.make_async_copy(m_own, m_one.at[t], recv_sem.at[3]).start()

    @pl.loop(1, 16)
    def _(k):
        remote(m_own, m_one.at[t], 3, {"space": near(k)[1]}).start()

    arrived(e_mid, 1)
    turn(e_mid, e_turn)
    send_far(e_turn, e_all, 4)
    arrived(u_mid, 0)
    turn(u_mid, u_turn)
    send_far(u_turn, u_all, 2)

    loads[11].wait()
    tall = lax.broadcasted_iota(jnp.int32, (32, 512), 1) // 16
    spread_t = tall == lax.broadcasted_iota(jnp.int32, (32, 512), 0)
    repeated = dot(v_skip[...], spread_t.astype(F32).astype(BF16))
    for n in range(4):
        skip_rows[n] = repeated[:, N * n : N * n + N]
    for i in range(CHANNELS):
        row = lanes([skip_rows[n, pl.ds(i, 16, stride=0), :] for n in range(4)])
        kron[16 * i : 16 * i + 16, :] = jnp.where(same, row, 0.0).astype(BF16)
    for j in range(0, 8, 2):
        pair = [v_cp[:, 16 * n : 16 * n + 16, :].reshape(512, N) for n in (j, j + 1)]
        mixed = dot(kron[...], lanes(pair))
        for n in range(2):
            v_mix[:, 16 * (j + n) : 16 * (j + n) + 16, :] = mixed[:, N * n : N * n + N].reshape(
                32, 16, N
            )

    arrived(e_all, 4)
    loads[12].wait()
    e_rounded = []

    def put_e(part, value):
        for block in range(4):
            e_own[block, 8 * part : 8 * part + 8, :] = value[8 * block : 8 * block + 8, :]
        e_rounded.append(value.astype(BF16).astype(F32))

    along_y(e_all, fy, rows, put_e)

    loads[13].wait()
    e_real, e_imag = e_rounded
    for i in range(CHANNELS):
        w_real = v_weight[0, i].astype(F32)
        w_imag = v_weight[1, i].astype(F32)
        real = w_real * e_real + w_imag * e_imag
        imag = w_real * e_imag - w_imag * e_real
        for part, value in enumerate((real, imag)):
            partial[part, 8 * i : 8 * i + 8, :] = (
                value[0:8] + value[8:16] + (value[16:24] + value[24:32])
            )
    lane = lax.broadcasted_iota(jnp.int32, (1, N), 1)
    zero_kz = jnp.logical_and(q == 0, lane < 32)
    scale = jnp.where(zero_kz, 1.0, 2.0).astype(F32) / float(N * N * N)
    block = k4_lanes(32)
    for part in range(2):
        value = partial[part, pl.ds(0, 32, stride=8), :]
        for j in range(1, 8):
            value = value + partial[part, pl.ds(j, 32, stride=8), :]
        value = value * scale
        for k4 in range(4):
            back_rows[part, pl.ds(k4, 32, stride=4), :] = jnp.where(block == k4, value, 0.0)
    loads[14].wait()
    back = halves(lanes([back_rows[0], back_rows[1]]))
    g_send[...] = product((iy[0], iy[1]), back, (1, 1))
    send_near(g_send, g_mid, 6)

    pltpu.make_async_copy(e_own.at[sample], e_batch.at[sample], recv_sem.at[7]).start()

    @pl.loop(1, BATCH)
    def _(k):
        peer = other(k)
        remote(e_own.at[peer], e_batch.at[sample], 7, {"batch": peer}).start()

    arrived(u_all, 2)

    def put_u(part, value):
        u_own[32 * part : 32 * part + 32, :] = value

    along_y(u_all, fy, rows, put_u)
    send_batch(u_own, u_batch, 5)

    arrived(m_one, 3)
    total = m_one[0]
    for n in range(1, 16):
        total = total + m_one[n]
    m_two_own[...] = total
    pltpu.make_async_copy(m_two_own, m_two.at[b], recv_sem.at[8]).start()

    @pl.loop(1, 8)
    def _(k):
        remote(m_two_own, m_two.at[b], 8, {"space": far(k)[1]}).start()

    arrived(g_mid, 6)
    turn(g_mid, g_turn)
    send_far(g_turn, g_all, 9)

    arrived(u_batch, 5)
    arrived(e_batch, 7)
    for i in range(CHANNELS):
        real = jnp.zeros((8, N), F32)
        imag = jnp.zeros((8, N), F32)
        for n in range(BATCH):
            u_real = u_batch[n, pl.ds(i, 8, stride=0), :]
            u_imag = u_batch[n, pl.ds(32 + i, 8, stride=0), :]
            e_r = e_batch[n, 0:8, :]
            e_i = e_batch[n, 8:16, :]
            real = real + (u_real * e_r + u_imag * e_i)
            imag = imag + (u_real * e_i - u_imag * e_r)
        v_spectral[0, i] = real * scale
        v_spectral[1, i] = imag * scale

    arrived(m_two, 8)
    total = m_two[0]
    for n in range(1, 8):
        total = total + m_two[n]
    m_three_own[...] = total
    send_batch(m_three_own, m_three, 10)

    arrived(m_three, 10)
    total = (m_three[0] + m_three[1] + (m_three[2] + m_three[3])) / math.sqrt(BATCH * N * N * N)
    for r in range(4):
        v_mixgrad[8 * r : 8 * r + 8, :] = total[:, 32 * r : 32 * r + 32]

    loads[15].wait()
    loads[16].wait()
    arrived(g_all, 9)
    v_grid[...] = g_all[...]

    left(u_send.at[0:240], 0)
    left(e_send.at[0:240], 1)
    left(u_turn.at[0:7], 2)
    left(m_one.at[0:15], 3)
    left(e_turn.at[0:7], 4)
    left(u_batch.at[0:3], 5)
    left(g_send.at[0:240], 6)
    left(e_own.at[0:3], 7)
    left(m_two.at[0:7], 8)
    left(g_turn.at[0:7], 9)
    left(m_three.at[0:3], 10)

def grid_kernel(
    v_grid, v_mix, ix, iz, v_spectral, v_mixgrad, out_hbm, spectral_hbm, mixgrad_hbm, v_out, sems
):
    copies = [
        pltpu.make_async_copy(v_spectral, spectral_hbm, sems.at[4]),
        pltpu.make_async_copy(v_mixgrad, mixgrad_hbm, sems.at[5]),
    ]
    for copy in copies:
        copy.start()
    for g in range(4):
        spectra = lanes(
            [
                v_grid[:, 8 * n : 8 * n + 8, 32 * g : 32 * g + 32].reshape(64, 32)
                for n in range(4)
            ]
        )
        high, low = halves(spectra)
        along_x = dot(ix[...], jnp.concatenate([high, low, high], axis=0))
        both = lanes([along_x[:N], along_x[N:]]).astype(BF16)
        for n in range(4):
            grid = dot(both, iz[:, 256 * n : 256 * n + 256])
            for r in range(2):
                i = 8 * g + 2 * n + r
                v_out[i] = (grid[:, N * r : N * r + N] + v_mix[i]).astype(BF16)
        copy = pltpu.make_async_copy(
            v_out.at[8 * g : 8 * g + 8], out_hbm.at[8 * g : 8 * g + 8], sems.at[g]
        )
        copy.start()
        copies.append(copy)
    for copy in copies:
        copy.wait()


def on_device(inputs, pre_act, cotangent, spectral_weight, skip_weight):
    field = (CHANNELS, N, N)
    tables = [jnp.asarray(v) for v in make_tables()]
    exchange = [
        pltpu.VMEM((256, N), F32), pltpu.VMEM((256, N), F32),
        pltpu.VMEM((8, 32, N), F32), pltpu.VMEM((8, 32, N), F32),
    ]
    anywhere = pl.BlockSpec(memory_space=pl.ANY)
    near = pl.BlockSpec(memory_space=pltpu.VMEM)
    spectral_type = jax.ShapeDtypeStruct((2, CHANNELS, 8, N), F32)
    skip_type = jax.ShapeDtypeStruct((CHANNELS, CHANNELS), F32)
    operands = [
        inputs.reshape(field), pre_act.reshape(field), cotangent.reshape(field),
        spectral_weight, skip_weight, *tables,
    ]
    stages = pl.pallas_call(
        spectral_kernel,
        out_shape=(
            jax.ShapeDtypeStruct((8, 32, N), F32),
            jax.ShapeDtypeStruct(field, F32),
            jax.ShapeDtypeStruct(tables[4].shape, BF16),
            jax.ShapeDtypeStruct(tables[5].shape, BF16),
            spectral_type,
            skip_type,
        ),
        in_specs=[anywhere] * 11,
        out_specs=(near,) * 6,
        scratch_shapes=[
            pltpu.VMEM(field, BF16), pltpu.VMEM(field, BF16), pltpu.VMEM(field, BF16),
            pltpu.VMEM((2, 32, 32, N), BF16), pltpu.VMEM((32, 32), BF16),
            *(pltpu.VMEM(v.shape, BF16) for v in tables[:4]),
            pltpu.VMEM(field, BF16),
            *exchange, *exchange, *exchange,
            pltpu.VMEM((64, N), F32), pltpu.VMEM((BATCH, 64, N), F32),
            pltpu.VMEM((4, 16, N), F32), pltpu.VMEM((BATCH, 16, N), F32),
            pltpu.VMEM((2, N, N), F32), pltpu.VMEM((2, 256, N), F32), pltpu.VMEM((2, N, N), F32),
            pltpu.VMEM((512, 512), F32), pltpu.VMEM((4, 256, N), F32),
            pltpu.VMEM((512, 512), BF16), pltpu.VMEM((4, 32, N), F32),
            pltpu.VMEM((8, N), F32), pltpu.VMEM((16, 8, N), F32),
            pltpu.VMEM((8, N), F32), pltpu.VMEM((8, 8, N), F32),
            pltpu.VMEM((8, N), F32), pltpu.VMEM((BATCH, 8, N), F32),
            pltpu.SemaphoreType.DMA((17,)),
            pltpu.SemaphoreType.DMA((11,)), pltpu.SemaphoreType.DMA((11,)),
        ],
        compiler_params=pltpu.CompilerParams(
            collective_id=0, has_side_effects=True, vmem_limit_bytes=40 * 2**20
        ),
    )(*(pltpu.with_memory_space_constraint(v, pltpu.HBM) for v in operands))
    grad_inputs, grad_spectral, grad_skip = pl.pallas_call(
        grid_kernel,
        out_shape=(jax.ShapeDtypeStruct(field, BF16), spectral_type, skip_type),
        in_specs=[near] * 6,
        out_specs=(anywhere,) * 3,
        scratch_shapes=[pltpu.VMEM(field, BF16), pltpu.SemaphoreType.DMA((6,))],
        compiler_params=pltpu.CompilerParams(vmem_limit_bytes=24 * 2**20),
    )(*stages)
    return grad_inputs.reshape(inputs.shape), grad_spectral, grad_skip


def solution(mesh):
    placed = (
        P("batch", None, None, "space", None),
        P("batch", None, None, "space", None),
        P("batch", None, None, "space", None),
        P(None, None, None, "space"),
        P(),
    )
    return jax.shard_map(
        on_device,
        mesh=mesh,
        in_specs=placed,
        out_specs=(P("batch", None, None, "space", None), P(None, None, "batch", "space"), P()),
        check_vma=False,
    )
```

```python
import math

import jax
import jax.numpy as jnp
import ml_dtypes
import numpy as np
from jax import lax
from jax.experimental import pallas as pl
from jax.experimental.pallas import tpu as pltpu
from jax.sharding import PartitionSpec as P

N = 128
MODES = 32
BATCH = 4
CHANNELS = 32
F32 = jnp.float32
BF16 = jnp.bfloat16
MESH = pl.DeviceIdType.MESH


def signed(index):
    return np.where(index < 16, index, index - 32)


def phases(points, orders):
    angles = np.mod(points[:, None] * orders[None, :], N) * (2.0 * math.pi / N)
    return np.cos(angles), np.sin(angles)


def bf16(table):
    return table.astype(np.float32).astype(ml_dtypes.bfloat16)


def split(table):
    high = bf16(table)
    return high, bf16(table - high.astype(np.float64))


def places():
    t = np.arange(16)
    return t // 4, t // 2 % 2, t % 2


def make_tables():
    points = np.arange(N)
    eye = np.eye(8)
    cos_z, sin_z = (v.reshape(N, 4, 4) for v in phases(points, np.arange(16)))
    fwd_z = np.stack([np.einsum("zqk,cd->czqdk", v, eye) for v in (cos_z, -sin_z)], axis=2)
    fwd_z = fwd_z.reshape(8 * N, 256)
    inv_z = np.stack([np.einsum("zqk,cd->qckdz", v, eye) for v in (cos_z, -sin_z)], axis=0)
    inv_z = inv_z.reshape(256, 8 * N)
    cos_x, sin_x = phases(points, signed(np.arange(32)))
    cos_x, sin_x = bf16(cos_x).astype(np.float64), bf16(sin_x).astype(np.float64)
    parts = np.stack([np.stack([cos_x, sin_x]), np.stack([-sin_x, cos_x])])
    parts = parts.reshape(2, 2, N, 2, 8, 2)
    fwd_x = np.transpose(parts, (3, 5, 0, 4, 1, 2)).reshape(64, 256)
    cos_x, sin_x = phases(points, signed(np.arange(32)))
    parts = np.stack([np.stack([cos_x, -sin_x]), np.stack([sin_x, cos_x])])
    inv_x = np.transpose(parts, (0, 2, 3, 1)).reshape(256, 64)
    q, a, h = places()
    y = a[None, :] * 64 + np.arange(8)[:, None] * 8 + h[None, :] * 4 + q[None, :]
    cos_y, sin_y = phases(y.reshape(-1), signed(np.arange(32)))
    cos_y, sin_y = cos_y.reshape(8, 16, 32), sin_y.reshape(8, 16, 32)
    parts = np.stack([np.stack([cos_y, sin_y]), np.stack([-sin_y, cos_y])])
    fwd_y = np.transpose(parts, (2, 3, 1, 0, 4))[:, :, :, :, None, :]
    fwd_y = np.broadcast_to(fwd_y, (8, 16, 2, 2, 4, 32)).reshape(256, 256)
    cos_y, sin_y = phases(points, signed(np.arange(32)))
    parts = np.stack([np.stack([cos_y, -sin_y]), np.stack([sin_y, cos_y])])
    inv_y = np.transpose(parts, (2, 0, 1, 3))[:, :, :, None, :]
    inv_y = np.broadcast_to(inv_y, (N, 2, 2, 4, 32)).reshape(256, 256)
    inv_x_high, inv_x_low = split(inv_x)
    inv_x = np.concatenate([inv_x_high, inv_x_high, inv_x_low], axis=1)
    fwd_y, inv_y = np.stack(split(fwd_y)), np.stack(split(inv_y))
    return bf16(fwd_z), bf16(fwd_x), fwd_y, inv_y, inv_x, bf16(inv_z)


def gelu_slope(values):
    normal_cdf = 0.5 * (1.0 + lax.erf(values * (1.0 / math.sqrt(2.0))))
    density = jnp.exp(-0.5 * values * values) * (1.0 / math.sqrt(2.0 * math.pi))
    return normal_cdf + values * density


def dot(left, right):
    return jnp.dot(left, right, preferred_element_type=F32)


def halves(value):
    high = value.astype(BF16)
    return high, (value - high.astype(F32)).astype(BF16)


def product(left, right, contracted):
    def one(first, second):
        return lax.dot_general(
            first, second, ((contracted[:1], contracted[1:]), ((), ())), preferred_element_type=F32
        )

    return one(left[0], right[0]) + (one(left[1], right[0]) + one(left[0], right[1]))


def lanes(blocks):
    return jnp.concatenate(blocks, axis=1)


def all_sections(field, table_z, table_x):
    planes = [
        jnp.concatenate([field[8 * g + j] for g in range(4)], axis=0) for j in range(8)
    ]
    along_z = dot(lanes(planes), table_z[...])
    both = jnp.concatenate(
        [
            lanes([along_z[N * g : N * g + N, N * part : N * part + N] for g in range(4)])
            for part in range(2)
        ],
        axis=0,
    ).astype(BF16)
    found = dot(table_x[...], both)
    return [found[:, N * g : N * g + N] for g in range(4)]


def to_blocks(sections, sent):
    for q in range(4):
        sent[64 * q : 64 * q + 64, :] = lanes([v[:, 32 * q : 32 * q + 32] for v in sections])


def turn(received, sent):
    for b in range(8):
        sent[b] = received[pl.ds(b, 32, stride=8), :]


def k4_lanes(rows):
    return lax.broadcasted_iota(jnp.int32, (rows, N), 1) // 32


def along_y(received, table_y, rows, put):
    both = product(
        halves(received[...].reshape(256, N)), (table_y[0], table_y[1]), (0, 0)
    )
    block = k4_lanes(32)
    for part in range(2):
        rows[part] = both[:, N * part : N * part + N]
        value = rows[part, pl.ds(0, 32, stride=4), :]
        for k4 in range(1, 4):
            value = jnp.where(block == k4, rows[part, pl.ds(k4, 32, stride=4), :], value)
        put(part, value)


def spectral_kernel(
    in_hbm, pre_hbm, cot_hbm, weight_hbm, skip_hbm,
    fz_hbm, fx_hbm, fy_hbm, iy_hbm, ix_hbm, iz_hbm,
    v_grid, v_mix, ix, iz, v_spectral, v_mixgrad,
    v_in, v_pre, v_cot, v_weight, v_skip, fz, fx, fy, iy,
    v_cp,
    u_send, u_mid, u_turn, u_all, e_send, e_mid, e_turn, e_all, g_send, g_all,
    u_own, u_batch, e_own, e_batch, rows, partial, back_rows,
    prod, prod_rows, kron, skip_rows, m_own, m_one, m_two_own, m_two, m_three_own, m_three,
    load_sem, send_sem, recv_sem,
):
    sample = lax.axis_index("batch")
    place = lax.axis_index("space")
    a = place // 64
    b = place // 8 % 8
    h = place // 4 % 2
    q = place % 4
    t = 4 * q + 2 * a + h

    def near(k):
        peer = (t + k) % 16
        return peer, peer // 2 % 2 * 64 + b * 8 + peer % 2 * 4 + peer // 4

    def near_first():
        z = place % 8
        for step in (4, 3, 5, 2, 6, 1, 7, 0):
            c = (z + step) % 8
            for side in (1 - a, a):
                if step or side is not a:
                    yield c % 4 * 4 + side * 2 + c // 4, side * 64 + b * 8 + c

    def far(k):
        peer = (b + k) % 8
        return peer, a * 64 + peer * 8 + h * 4 + q

    def far_first():
        return [far(k) for k in (4, 3, 5, 2, 6, 1, 7)]

    def other(k):
        return (sample + k) % BATCH

    barrier = pltpu.get_barrier_semaphore()
    for _, where in [*near_first(), *far_first()]:
        pl.semaphore_signal(barrier, inc=1, device_id={"space": where}, device_id_type=MESH)

    @pl.loop(1, BATCH)
    def _(k):
        pl.semaphore_signal(barrier, inc=1, device_id={"batch": other(k)}, device_id_type=MESH)

    def group(ref, g):
        return ref.at[8 * g : 8 * g + 8]

    pairs = []
    for g in range(4):
        pairs += [(group(src, g), group(dst, g)) for src, dst in ((pre_hbm, v_pre), (cot_hbm, v_cot))]
    pairs += [
        (fz_hbm, fz), (fx_hbm, fx), (in_hbm, v_in), (skip_hbm, v_skip), (fy_hbm, fy), (weight_hbm, v_weight),
        (iy_hbm, iy), (ix_hbm, ix), (iz_hbm, iz),
    ]
    loads = [
        pltpu.make_async_copy(src, dst, load_sem.at[n]) for n, (src, dst) in enumerate(pairs)
    ]
    for copy in loads[:10]:
        copy.start()

    def remote(src, dst, n, where):
        return pltpu.make_async_remote_copy(
            src_ref=src, dst_ref=dst, send_sem=send_sem.at[n], recv_sem=recv_sem.at[n],
            device_id=where, device_id_type=MESH,
        )

    def rows16(ref, slot):
        return ref.at[pl.ds(pl.multiple_of(slot * 16, 16), 16), :]

    def send_near(src, dst, n):
        for peer, where in near_first():
            remote(rows16(src, peer), rows16(dst, t), n, {"space": where}).start()
        pltpu.make_async_copy(rows16(src, t), rows16(dst, t), recv_sem.at[n]).start()

    def send_far(src, dst, n):
        for peer, where in far_first():
            remote(src.at[peer], dst.at[b], n, {"space": where}).start()
        pltpu.make_async_copy(src.at[b], dst.at[b], recv_sem.at[n]).start()

    def distant_first(index):
        return 4 + (index + 1) // 2 * (1 - 2 * (index % 2))

    def send_all(src, dst, n):
        mine = dst.at[pl.ds(pl.multiple_of(64 * q + place // 4 * 2, 2), 2), :]

        @pl.loop(0, N - 1)
        def _(k):
            y = (b + distant_first(k // 16)) % 8
            z = (place + distant_first(k // 2 % 8)) % 8
            where = (a + 1 + k % 2) % 2 * 64 + y * 8 + z
            rows = src.at[pl.ds(pl.multiple_of(where * 2, 2), 2), :]
            remote(rows, mine, n, {"space": where}).start()

        rows = src.at[pl.ds(pl.multiple_of(place * 2, 2), 2), :]
        pltpu.make_async_copy(rows, mine, recv_sem.at[n]).start()

    def send_batch(src, dst, n):
        pltpu.make_async_copy(src, dst.at[sample], recv_sem.at[n]).start()

        @pl.loop(1, BATCH)
        def _(k):
            remote(src, dst.at[sample], n, {"batch": other(k)}).start()

    def arrived(ref, n):
        pltpu.make_async_copy(ref, ref, recv_sem.at[n]).wait()

    def left(ref, n):
        pltpu.make_async_copy(ref, ref, send_sem.at[n]).wait()

    for g in range(4):
        loads[2 * g].wait()
        loads[2 * g + 1].wait()
        for c in range(8 * g, 8 * g + 8):
            slope = gelu_slope(v_pre[c].astype(F32))
            v_cp[c] = (v_cot[c].astype(F32) * slope).astype(BF16)
    for copy in loads[10:]:
        copy.start()
    loads[8].wait()
    loads[9].wait()
    sections = all_sections(v_cp, fz, fx)
    to_blocks(sections, e_send)
    pl.semaphore_wait(barrier, 15 + 7 + BATCH - 1)
    send_near(e_send, e_mid, 1)

    loads[10].wait()
    to_blocks(all_sections(v_in, fz, fx), u_send)
    send_near(u_send, u_mid, 0)

    chunks = range(8)
    prod[...] = lax.dot_general(
        lanes([v_in[:, 16 * j : 16 * j + 16, :].reshape(512, N) for j in chunks]),
        lanes([v_cp[:, 16 * j : 16 * j + 16, :].reshape(512, N) for j in chunks]),
        (((1,), (1,)), ((), ())),
        preferred_element_type=F32,
    )
    row16 = lax.broadcasted_iota(jnp.int32, (16, 512), 0)
    column = lax.broadcasted_iota(jnp.int32, (16, 512), 1)
    same = row16 == column % 16
    for i in range(CHANNELS):
        kept = jnp.where(same, prod[16 * i : 16 * i + 16, :], 0.0)
        kept = kept[:8] + kept[8:]
        for n in range(4):
            prod_rows[n, 8 * i : 8 * i + 8, :] = kept[:, N * n : N * n + N]
    summed = []
    for n in range(4):
        value = prod_rows[n, pl.ds(0, 32, stride=8), :]
        for j in range(1, 8):
            value = value + prod_rows[n, pl.ds(j, 32, stride=8), :]
        summed.append(value)
    summed = lanes(summed)
    wide = lax.broadcasted_iota(jnp.int32, (512, 32), 0) // 16
    spread = wide == lax.broadcasted_iota(jnp.int32, (512, 32), 1)
    own = jnp.dot(
        summed, spread.astype(F32), precision=lax.Precision.HIGHEST, preferred_element_type=F32
    )
    m_own[...] = lanes([own[8 * r : 8 * r + 8, :] for r in range(4)])

    pltpu.make_async_copy(m_own, m_one.at[t], recv_sem.at[3]).start()

    @pl.loop(1, 16)
    def _(k):
        remote(m_own, m_one.at[t], 3, {"space": near(k)[1]}).start()

    arrived(e_mid, 1)
    turn(e_mid, e_turn)
    send_far(e_turn, e_all, 4)
    arrived(u_mid, 0)
    turn(u_mid, u_turn)
    send_far(u_turn, u_all, 2)

    loads[11].wait()
    tall = lax.broadcasted_iota(jnp.int32, (32, 512), 1) // 16
    spread_t = tall == lax.broadcasted_iota(jnp.int32, (32, 512), 0)
    repeated = dot(v_skip[...], spread_t.astype(F32).astype(BF16))
    for n in range(4):
        skip_rows[n] = repeated[:, N * n : N * n + N]
    for i in range(CHANNELS):
        row = lanes([skip_rows[n, pl.ds(i, 16, stride=0), :] for n in range(4)])
        kron[16 * i : 16 * i + 16, :] = jnp.where(same, row, 0.0).astype(BF16)
    for j in range(0, 8, 2):
        pair = [v_cp[:, 16 * n : 16 * n + 16, :].reshape(512, N) for n in (j, j + 1)]
        mixed = dot(kron[...], lanes(pair))
        for n in range(2):
            v_mix[:, 16 * (j + n) : 16 * (j + n) + 16, :] = mixed[:, N * n : N * n + N].reshape(
                32, 16, N
            )

    arrived(m_one, 3)
    total = m_one[0]
    for n in range(1, 16):
        total = total + m_one[n]
    m_two_own[...] = total
    pltpu.make_async_copy(m_two_own, m_two.at[b], recv_sem.at[8]).start()

    @pl.loop(1, 8)
    def _(k):
        remote(m_two_own, m_two.at[b], 8, {"space": far(k)[1]}).start()

    arrived(e_all, 4)
    loads[12].wait()
    e_rounded = []

    def put_e(part, value):
        for block in range(4):
            e_own[block, 8 * part : 8 * part + 8, :] = value[8 * block : 8 * block + 8, :]
        e_rounded.append(value.astype(BF16).astype(F32))

    along_y(e_all, fy, rows, put_e)

    loads[13].wait()
    e_real, e_imag = e_rounded
    for i in range(CHANNELS):
        w_real = v_weight[0, i].astype(F32)
        w_imag = v_weight[1, i].astype(F32)
        real = w_real * e_real + w_imag * e_imag
        imag = w_real * e_imag - w_imag * e_real
        for part, value in enumerate((real, imag)):
            partial[part, 8 * i : 8 * i + 8, :] = (
                value[0:8] + value[8:16] + (value[16:24] + value[24:32])
            )
    lane = lax.broadcasted_iota(jnp.int32, (1, N), 1)
    zero_kz = jnp.logical_and(q == 0, lane < 32)
    scale = jnp.where(zero_kz, 1.0, 2.0).astype(F32) / float(N * N * N)
    block = k4_lanes(32)
    for part in range(2):
        value = partial[part, pl.ds(0, 32, stride=8), :]
        for j in range(1, 8):
            value = value + partial[part, pl.ds(j, 32, stride=8), :]
        value = value * scale
        for k4 in range(4):
            back_rows[part, pl.ds(k4, 32, stride=4), :] = jnp.where(block == k4, value, 0.0)
    loads[14].wait()
    back = halves(lanes([back_rows[0], back_rows[1]]))
    g_send[...] = product((iy[0], iy[1]), back, (1, 1))
    send_all(g_send, g_all, 9)

    pltpu.make_async_copy(e_own.at[sample], e_batch.at[sample], recv_sem.at[7]).start()

    @pl.loop(1, BATCH)
    def _(k):
        peer = other(k)
        remote(e_own.at[peer], e_batch.at[sample], 7, {"batch": peer}).start()

    arrived(u_all, 2)

    def put_u(part, value):
        u_own[32 * part : 32 * part + 32, :] = value

    along_y(u_all, fy, rows, put_u)
    send_batch(u_own, u_batch, 5)

    arrived(m_two, 8)
    total = m_two[0]
    for n in range(1, 8):
        total = total + m_two[n]
    m_three_own[...] = total
    send_batch(m_three_own, m_three, 10)

    arrived(u_batch, 5)
    arrived(e_batch, 7)
    for i in range(CHANNELS):
        real = jnp.zeros((8, N), F32)
        imag = jnp.zeros((8, N), F32)
        for n in range(BATCH):
            u_real = u_batch[n, pl.ds(i, 8, stride=0), :]
            u_imag = u_batch[n, pl.ds(32 + i, 8, stride=0), :]
            e_r = e_batch[n, 0:8, :]
            e_i = e_batch[n, 8:16, :]
            real = real + (u_real * e_r + u_imag * e_i)
            imag = imag + (u_real * e_i - u_imag * e_r)
        v_spectral[0, i] = real * scale
        v_spectral[1, i] = imag * scale

    arrived(m_three, 10)
    total = (m_three[0] + m_three[1] + (m_three[2] + m_three[3])) / math.sqrt(BATCH * N * N * N)
    for r in range(4):
        v_mixgrad[8 * r : 8 * r + 8, :] = total[:, 32 * r : 32 * r + 32]

    loads[15].wait()
    loads[16].wait()
    arrived(g_all, 9)
    v_grid[...] = g_all[...]

    left(u_send.at[0:240], 0)
    left(e_send.at[0:240], 1)
    left(u_turn.at[0:7], 2)
    left(m_one.at[0:15], 3)
    left(e_turn.at[0:7], 4)
    left(u_batch.at[0:3], 5)
    left(e_own.at[0:3], 7)
    left(m_two.at[0:7], 8)
    left(g_send.at[0:254], 9)
    left(m_three.at[0:3], 10)

def grid_kernel(
    v_grid, v_mix, ix, iz, v_spectral, v_mixgrad, out_hbm, spectral_hbm, mixgrad_hbm, v_out, sems
):
    copies = [
        pltpu.make_async_copy(v_spectral, spectral_hbm, sems.at[4]),
        pltpu.make_async_copy(v_mixgrad, mixgrad_hbm, sems.at[5]),
    ]
    for copy in copies:
        copy.start()
    stacked = []
    for g in range(4):
        spectra = lanes([v_grid[64 * n : 64 * n + 64, 32 * g : 32 * g + 32] for n in range(4)])
        high, low = halves(spectra)
        along_x = dot(ix[...], jnp.concatenate([high, low, high], axis=0))
        stacked.append(lanes([along_x[:N], along_x[N:]]).astype(BF16))
    stacked = jnp.concatenate(stacked, axis=0)
    for n in range(4):
        grid = dot(stacked, iz[:, 256 * n : 256 * n + 256])
        for g in range(4):
            for r in range(2):
                i = 8 * g + 2 * n + r
                block = grid[N * g : N * g + N, N * r : N * r + N]
                v_out[g, 2 * n + r] = (block + v_mix[i]).astype(BF16)
        copy = pltpu.make_async_copy(
            v_out.at[:, 2 * n : 2 * n + 2], out_hbm.at[:, 2 * n : 2 * n + 2], sems.at[n]
        )
        copy.start()
        copies.append(copy)
    for copy in copies:
        copy.wait()


def on_device(inputs, pre_act, cotangent, spectral_weight, skip_weight):
    field = (CHANNELS, N, N)
    tables = [jnp.asarray(v) for v in make_tables()]
    exchange = [
        pltpu.VMEM((256, N), F32), pltpu.VMEM((256, N), F32),
        pltpu.VMEM((8, 32, N), F32), pltpu.VMEM((8, 32, N), F32),
    ]
    anywhere = pl.BlockSpec(memory_space=pl.ANY)
    near = pl.BlockSpec(memory_space=pltpu.VMEM)
    spectral_type = jax.ShapeDtypeStruct((2, CHANNELS, 8, N), F32)
    skip_type = jax.ShapeDtypeStruct((CHANNELS, CHANNELS), F32)
    operands = [
        inputs.reshape(field), pre_act.reshape(field), cotangent.reshape(field),
        spectral_weight, skip_weight, *tables,
    ]
    stages = pl.pallas_call(
        spectral_kernel,
        out_shape=(
            jax.ShapeDtypeStruct((256, N), F32),
            jax.ShapeDtypeStruct(field, F32),
            jax.ShapeDtypeStruct(tables[4].shape, BF16),
            jax.ShapeDtypeStruct(tables[5].shape, BF16),
            spectral_type,
            skip_type,
        ),
        in_specs=[anywhere] * 11,
        out_specs=(near,) * 6,
        scratch_shapes=[
            pltpu.VMEM(field, BF16), pltpu.VMEM(field, BF16), pltpu.VMEM(field, BF16),
            pltpu.VMEM((2, 32, 32, N), BF16), pltpu.VMEM((32, 32), BF16),
            *(pltpu.VMEM(v.shape, BF16) for v in tables[:4]),
            pltpu.VMEM(field, BF16),
            *exchange, *exchange, pltpu.VMEM((256, N), F32), pltpu.VMEM((256, N), F32),
            pltpu.VMEM((64, N), F32), pltpu.VMEM((BATCH, 64, N), F32),
            pltpu.VMEM((4, 16, N), F32), pltpu.VMEM((BATCH, 16, N), F32),
            pltpu.VMEM((2, N, N), F32), pltpu.VMEM((2, 256, N), F32), pltpu.VMEM((2, N, N), F32),
            pltpu.VMEM((512, 512), F32), pltpu.VMEM((4, 256, N), F32),
            pltpu.VMEM((512, 512), BF16), pltpu.VMEM((4, 32, N), F32),
            pltpu.VMEM((8, N), F32), pltpu.VMEM((16, 8, N), F32),
            pltpu.VMEM((8, N), F32), pltpu.VMEM((8, 8, N), F32),
            pltpu.VMEM((8, N), F32), pltpu.VMEM((BATCH, 8, N), F32),
            pltpu.SemaphoreType.DMA((17,)),
            pltpu.SemaphoreType.DMA((11,)), pltpu.SemaphoreType.DMA((11,)),
        ],
        compiler_params=pltpu.CompilerParams(
            collective_id=0, has_side_effects=True, vmem_limit_bytes=40 * 2**20
        ),
    )(*(pltpu.with_memory_space_constraint(v, pltpu.HBM) for v in operands))
    grad_inputs, grad_spectral, grad_skip = pl.pallas_call(
        grid_kernel,
        out_shape=(jax.ShapeDtypeStruct((4, 8, N, N), BF16), spectral_type, skip_type),
        in_specs=[near] * 6,
        out_specs=(anywhere,) * 3,
        scratch_shapes=[pltpu.VMEM((4, 8, N, N), BF16), pltpu.SemaphoreType.DMA((6,))],
        compiler_params=pltpu.CompilerParams(vmem_limit_bytes=24 * 2**20),
    )(*stages)
    return grad_inputs.reshape(inputs.shape), grad_spectral, grad_skip


def solution(mesh):
    placed = (
        P("batch", None, None, "space", None),
        P("batch", None, None, "space", None),
        P("batch", None, None, "space", None),
        P(None, None, None, "space"),
        P(),
    )
    return jax.shard_map(
        on_device,
        mesh=mesh,
        in_specs=placed,
        out_specs=(P("batch", None, None, "space", None), P(None, None, "batch", "space"), P()),
        check_vma=False,
    )
```

```python
import math

import jax
import jax.numpy as jnp
import ml_dtypes
import numpy as np
from jax import lax
from jax.experimental import pallas as pl
from jax.experimental.pallas import tpu as pltpu
from jax.sharding import PartitionSpec as P

N = 128
MODES = 32
BATCH = 4
CHANNELS = 32
F32 = jnp.float32
BF16 = jnp.bfloat16
MESH = pl.DeviceIdType.MESH


def signed(index):
    return np.where(index < 16, index, index - 32)


def phases(points, orders):
    angles = np.mod(points[:, None] * orders[None, :], N) * (2.0 * math.pi / N)
    return np.cos(angles), np.sin(angles)


def bf16(table):
    return table.astype(np.float32).astype(ml_dtypes.bfloat16)


def split(table):
    high = bf16(table)
    return high, bf16(table - high.astype(np.float64))


def places():
    t = np.arange(16)
    return t // 4, t // 2 % 2, t % 2


def make_tables():
    points = np.arange(N)
    eye = np.eye(8)
    cos_z, sin_z = (v.reshape(N, 4, 4) for v in phases(points, np.arange(16)))
    fwd_z = np.stack([np.einsum("zqk,cd->czqdk", v, eye) for v in (cos_z, -sin_z)], axis=2)
    fwd_z = fwd_z.reshape(8 * N, 256)
    inv_z = np.stack([np.einsum("zqk,cd->qckdz", v, eye) for v in (cos_z, -sin_z)], axis=0)
    inv_z = inv_z.reshape(256, 8 * N)
    cos_x, sin_x = phases(points, signed(np.arange(32)))
    cos_x, sin_x = bf16(cos_x).astype(np.float64), bf16(sin_x).astype(np.float64)
    parts = np.stack([np.stack([cos_x, sin_x]), np.stack([-sin_x, cos_x])])
    parts = parts.reshape(2, 2, N, 2, 8, 2)
    fwd_x = np.transpose(parts, (3, 5, 0, 4, 1, 2)).reshape(64, 256)
    cos_x, sin_x = phases(points, signed(np.arange(32)))
    parts = np.stack([np.stack([cos_x, -sin_x]), np.stack([sin_x, cos_x])]).reshape(2, 2, N, 2, 8, 2)
    inv_x = np.transpose(parts, (0, 2, 4, 3, 5, 1)).reshape(256, 64)
    q, a, h = places()
    y = a[None, :] * 64 + np.arange(8)[:, None] * 8 + h[None, :] * 4 + q[None, :]
    cos_y, sin_y = phases(y.reshape(-1), signed(np.arange(32)))
    cos_y, sin_y = cos_y.reshape(8, 16, 32), sin_y.reshape(8, 16, 32)
    parts = np.stack([np.stack([cos_y, sin_y]), np.stack([-sin_y, cos_y])])
    fwd_y = np.transpose(parts, (2, 3, 1, 0, 4))[:, :, :, :, None, :]
    fwd_y = np.broadcast_to(fwd_y, (8, 16, 2, 2, 4, 32)).reshape(256, 256)
    parts = np.stack([np.stack([cos_y, -sin_y]), np.stack([sin_y, cos_y])])
    inv_y = np.transpose(parts, (3, 0, 2, 1, 4))[:, :, :, :, None, :]
    inv_y = np.broadcast_to(inv_y, (16, 2, 8, 2, 4, 32)).reshape(256, 256)
    inv_x_high, inv_x_low = split(inv_x)
    inv_x = np.concatenate([inv_x_high, inv_x_high, inv_x_low], axis=1)
    fwd_y, inv_y = np.stack(split(fwd_y)), np.stack(split(inv_y))
    return bf16(fwd_z), bf16(fwd_x), fwd_y, inv_y, inv_x, bf16(inv_z)


def gelu_slope(values):
    normal_cdf = 0.5 * (1.0 + lax.erf(values * (1.0 / math.sqrt(2.0))))
    density = jnp.exp(-0.5 * values * values) * (1.0 / math.sqrt(2.0 * math.pi))
    return normal_cdf + values * density


def dot(left, right):
    return jnp.dot(left, right, preferred_element_type=F32)


def halves(value):
    high = value.astype(BF16)
    return high, (value - high.astype(F32)).astype(BF16)


def product(left, right, contracted):
    def one(first, second):
        return lax.dot_general(
            first, second, ((contracted[:1], contracted[1:]), ((), ())), preferred_element_type=F32
        )

    return one(left[0], right[0]) + (one(left[1], right[0]) + one(left[0], right[1]))


def lanes(blocks):
    return jnp.concatenate(blocks, axis=1)


def all_sections(field, table_z, table_x):
    planes = [
        jnp.concatenate([field[8 * g + j] for g in range(4)], axis=0) for j in range(8)
    ]
    along_z = dot(lanes(planes), table_z[...])
    both = jnp.concatenate(
        [
            lanes([along_z[N * g : N * g + N, N * part : N * part + N] for g in range(4)])
            for part in range(2)
        ],
        axis=0,
    ).astype(BF16)
    found = dot(table_x[...], both)
    return [found[:, N * g : N * g + N] for g in range(4)]


def to_blocks(sections, sent):
    for q in range(4):
        sent[64 * q : 64 * q + 64, :] = lanes([v[:, 32 * q : 32 * q + 32] for v in sections])


def turn(received, sent):
    for b in range(8):
        sent[b] = received[pl.ds(b, 32, stride=8), :]


def cross(received, sent):
    for t in range(16):
        for part in range(2):
            sent[16 * t + 8 * part : 16 * t + 8 * part + 8, :] = received[
                pl.ds(2 * t + part, 8, stride=32), :
            ]


def k4_lanes(rows):
    return lax.broadcasted_iota(jnp.int32, (rows, N), 1) // 32


def along_y(received, table_y, rows, put):
    both = product(
        halves(received[...]), (table_y[0], table_y[1]), (0, 0)
    )
    block = k4_lanes(32)
    for part in range(2):
        rows[part] = both[:, N * part : N * part + N]
        value = rows[part, pl.ds(0, 32, stride=4), :]
        for k4 in range(1, 4):
            value = jnp.where(block == k4, rows[part, pl.ds(k4, 32, stride=4), :], value)
        put(part, value)


def spectral_kernel(
    in_hbm, pre_hbm, cot_hbm, weight_hbm, skip_hbm,
    fz_hbm, fx_hbm, fy_hbm, iy_hbm, ix_hbm, iz_hbm,
    v_grid, v_mix, ix, iz, v_spectral, v_mixgrad,
    v_in, v_pre, v_cot, v_weight, v_skip, fz, fx, fy, iy,
    v_cp,
    u_send, u_mid, u_turn, u_all, u_near, u_last, e_send, e_mid, e_turn, e_all, g_send, g_mid, g_turn, g_all,
    u_own, u_batch, e_own, e_batch, rows, partial, back_rows,
    prod, prod_rows, kron, skip_rows, m_own, m_one, m_two_own, m_two, m_three_own, m_three,
    load_sem, send_sem, recv_sem,
):
    sample = lax.axis_index("batch")
    place = lax.axis_index("space")
    a = place // 64
    b = place // 8 % 8
    h = place // 4 % 2
    q = place % 4
    t = 4 * q + 2 * a + h

    def near(k):
        peer = (t + k) % 16
        return peer, peer // 2 % 2 * 64 + b * 8 + peer % 2 * 4 + peer // 4

    def near_first():
        z = place % 8
        for step in (4, 3, 5, 2, 6, 1, 7, 0):
            c = (z + step) % 8
            for side in (1 - a, a):
                if step or side is not a:
                    yield c % 4 * 4 + side * 2 + c // 4, side * 64 + b * 8 + c

    def far(k):
        peer = (b + k) % 8
        return peer, a * 64 + peer * 8 + h * 4 + q

    def far_first():
        return [far(k) for k in (4, 3, 5, 2, 6, 1, 7)]

    def other(k):
        return (sample + k) % BATCH

    barrier = pltpu.get_barrier_semaphore()
    for _, where in [*near_first(), *far_first()]:
        pl.semaphore_signal(barrier, inc=1, device_id={"space": where}, device_id_type=MESH)

    @pl.loop(1, BATCH)
    def _(k):
        pl.semaphore_signal(barrier, inc=1, device_id={"batch": other(k)}, device_id_type=MESH)

    def group(ref, g):
        return ref.at[8 * g : 8 * g + 8]

    pairs = []
    for g in range(4):
        pairs += [(group(src, g), group(dst, g)) for src, dst in ((pre_hbm, v_pre), (cot_hbm, v_cot))]
    pairs += [
        (fz_hbm, fz), (fx_hbm, fx), (in_hbm, v_in), (skip_hbm, v_skip), (fy_hbm, fy), (weight_hbm, v_weight),
        (iy_hbm, iy), (ix_hbm, ix), (iz_hbm, iz),
    ]
    loads = [
        pltpu.make_async_copy(src, dst, load_sem.at[n]) for n, (src, dst) in enumerate(pairs)
    ]
    for copy in loads[:10]:
        copy.start()

    def remote(src, dst, n, where):
        return pltpu.make_async_remote_copy(
            src_ref=src, dst_ref=dst, send_sem=send_sem.at[n], recv_sem=recv_sem.at[n],
            device_id=where, device_id_type=MESH,
        )

    def rows16(ref, slot):
        return ref.at[pl.ds(pl.multiple_of(slot * 16, 16), 16), :]

    def send_near(src, dst, n):
        for peer, where in near_first():
            remote(rows16(src, peer), rows16(dst, t), n, {"space": where}).start()
        pltpu.make_async_copy(rows16(src, t), rows16(dst, t), recv_sem.at[n]).start()

    def send_far(src, dst, n):
        mine = dst.at[pl.ds(pl.multiple_of(b * 32, 32), 32), :]
        for peer, where in far_first():
            remote(src.at[peer], mine, n, {"space": where}).start()
        pltpu.make_async_copy(src.at[b], mine, recv_sem.at[n]).start()

    def send_batch(src, dst, n):
        pltpu.make_async_copy(src, dst.at[sample], recv_sem.at[n]).start()

        @pl.loop(1, BATCH)
        def _(k):
            remote(src, dst.at[sample], n, {"batch": other(k)}).start()

    def arrived(ref, n):
        pltpu.make_async_copy(ref, ref, recv_sem.at[n]).wait()

    def left(ref, n):
        pltpu.make_async_copy(ref, ref, send_sem.at[n]).wait()

    for g in range(4):
        loads[2 * g].wait()
        loads[2 * g + 1].wait()
        for c in range(8 * g, 8 * g + 8):
            slope = gelu_slope(v_pre[c].astype(F32))
            v_cp[c] = (v_cot[c].astype(F32) * slope).astype(BF16)
    for copy in loads[10:]:
        copy.start()
    loads[8].wait()
    loads[9].wait()
    sections = all_sections(v_cp, fz, fx)
    to_blocks(sections, e_send)
    pl.semaphore_wait(barrier, 15 + 7 + BATCH - 1)
    send_near(e_send, e_mid, 1)

    loads[10].wait()
    to_blocks(all_sections(v_in, fz, fx), u_send)
    turn(u_send, u_turn)
    send_far(u_turn, u_mid, 0)

    chunks = range(8)
    prod[...] = lax.dot_general(
        lanes([v_in[:, 16 * j : 16 * j + 16, :].reshape(512, N) for j in chunks]),
        lanes([v_cp[:, 16 * j : 16 * j + 16, :].reshape(512, N) for j in chunks]),
        (((1,), (1,)), ((), ())),
        preferred_element_type=F32,
    )
    row16 = lax.broadcasted_iota(jnp.int32, (16, 512), 0)
    column = lax.broadcasted_iota(jnp.int32, (16, 512), 1)
    same = row16 == column % 16
    for i in range(CHANNELS):
        kept = jnp.where(same, prod[16 * i : 16 * i + 16, :], 0.0)
        kept = kept[:8] + kept[8:]
        for n in range(4):
            prod_rows[n, 8 * i : 8 * i + 8, :] = kept[:, N * n : N * n + N]
    summed = []
    for n in range(4):
        value = prod_rows[n, pl.ds(0, 32, stride=8), :]
        for j in range(1, 8):
            value = value + prod_rows[n, pl.ds(j, 32, stride=8), :]
        summed.append(value)
    summed = lanes(summed)
    wide = lax.broadcasted_iota(jnp.int32, (512, 32), 0) // 16
    spread = wide == lax.broadcasted_iota(jnp.int32, (512, 32), 1)
    own = jnp.dot(
        summed, spread.astype(F32), precision=lax.Precision.HIGHEST, preferred_element_type=F32
    )
    m_own[...] = lanes([own[8 * r : 8 * r + 8, :] for r in range(4)])

    pltpu.make_async_copy(m_own, m_one.at[t], recv_sem.at[3]).start()

    @pl.loop(1, 16)
    def _(k):
        remote(m_own, m_one.at[t], 3, {"space": near(k)[1]}).start()

    arrived(e_mid, 1)
    turn(e_mid, e_turn)
    send_far(e_turn, e_all, 4)
    arrived(u_mid, 0)
    cross(u_mid, u_near)
    send_near(u_near, u_last, 2)

    loads[11].wait()
    tall = lax.broadcasted_iota(jnp.int32, (32, 512), 1) // 16
    spread_t = tall == lax.broadcasted_iota(jnp.int32, (32, 512), 0)
    repeated = dot(v_skip[...], spread_t.astype(F32).astype(BF16))
    for n in range(4):
        skip_rows[n] = repeated[:, N * n : N * n + N]
    for i in range(CHANNELS):
        row = lanes([skip_rows[n, pl.ds(i, 16, stride=0), :] for n in range(4)])
        kron[16 * i : 16 * i + 16, :] = jnp.where(same, row, 0.0).astype(BF16)
    for j in range(0, 8, 2):
        pair = [v_cp[:, 16 * n : 16 * n + 16, :].reshape(512, N) for n in (j, j + 1)]
        mixed = dot(kron[...], lanes(pair))
        for n in range(2):
            v_mix[:, 16 * (j + n) : 16 * (j + n) + 16, :] = mixed[:, N * n : N * n + N].reshape(
                32, 16, N
            )

    arrived(m_one, 3)
    total = m_one[0]
    for n in range(1, 16):
        total = total + m_one[n]
    m_two_own[...] = total
    pltpu.make_async_copy(m_two_own, m_two.at[b], recv_sem.at[8]).start()

    @pl.loop(1, 8)
    def _(k):
        remote(m_two_own, m_two.at[b], 8, {"space": far(k)[1]}).start()

    arrived(e_all, 4)
    loads[12].wait()
    e_rounded = []

    def put_e(part, value):
        for block in range(4):
            e_own[block, 8 * part : 8 * part + 8, :] = value[8 * block : 8 * block + 8, :]
        e_rounded.append(value.astype(BF16).astype(F32))

    along_y(e_all, fy, rows, put_e)

    loads[13].wait()
    e_real, e_imag = e_rounded
    for i in range(CHANNELS):
        w_real = v_weight[0, i].astype(F32)
        w_imag = v_weight[1, i].astype(F32)
        real = w_real * e_real + w_imag * e_imag
        imag = w_real * e_imag - w_imag * e_real
        for part, value in enumerate((real, imag)):
            partial[part, 8 * i : 8 * i + 8, :] = (
                value[0:8] + value[8:16] + (value[16:24] + value[24:32])
            )
    lane = lax.broadcasted_iota(jnp.int32, (1, N), 1)
    zero_kz = jnp.logical_and(q == 0, lane < 32)
    scale = jnp.where(zero_kz, 1.0, 2.0).astype(F32) / float(N * N * N)
    block = k4_lanes(32)
    for part in range(2):
        value = partial[part, pl.ds(0, 32, stride=8), :]
        for j in range(1, 8):
            value = value + partial[part, pl.ds(j, 32, stride=8), :]
        value = value * scale
        for k4 in range(4):
            back_rows[part, pl.ds(k4, 32, stride=4), :] = jnp.where(block == k4, value, 0.0)
    loads[14].wait()
    back = halves(lanes([back_rows[0], back_rows[1]]))
    g_send[...] = product((iy[0], iy[1]), back, (1, 1))
    send_near(g_send, g_mid, 6)

    pltpu.make_async_copy(e_own.at[sample], e_batch.at[sample], recv_sem.at[7]).start()

    @pl.loop(1, BATCH)
    def _(k):
        peer = other(k)
        remote(e_own.at[peer], e_batch.at[sample], 7, {"batch": peer}).start()

    arrived(u_last, 2)
    for n in range(8):
        u_all[32 * n : 32 * n + 32, :] = u_last[pl.ds(n, 32, stride=8), :]

    def put_u(part, value):
        u_own[32 * part : 32 * part + 32, :] = value

    along_y(u_all, fy, rows, put_u)
    send_batch(u_own, u_batch, 5)

    arrived(m_two, 8)
    total = m_two[0]
    for n in range(1, 8):
        total = total + m_two[n]
    m_three_own[...] = total
    send_batch(m_three_own, m_three, 10)

    arrived(g_mid, 6)
    turn(g_mid, g_turn)
    send_far(g_turn, g_all, 9)

    arrived(u_batch, 5)
    arrived(e_batch, 7)
    for i in range(CHANNELS):
        real = jnp.zeros((8, N), F32)
        imag = jnp.zeros((8, N), F32)
        for n in range(BATCH):
            u_real = u_batch[n, pl.ds(i, 8, stride=0), :]
            u_imag = u_batch[n, pl.ds(32 + i, 8, stride=0), :]
            e_r = e_batch[n, 0:8, :]
            e_i = e_batch[n, 8:16, :]
            real = real + (u_real * e_r + u_imag * e_i)
            imag = imag + (u_real * e_i - u_imag * e_r)
        v_spectral[0, i] = real * scale
        v_spectral[1, i] = imag * scale

    arrived(m_three, 10)
    total = (m_three[0] + m_three[1] + (m_three[2] + m_three[3])) / math.sqrt(BATCH * N * N * N)
    for r in range(4):
        v_mixgrad[8 * r : 8 * r + 8, :] = total[:, 32 * r : 32 * r + 32]

    loads[15].wait()
    loads[16].wait()
    arrived(g_all, 9)
    v_grid[...] = g_all[...]

    left(u_turn.at[0:7], 0)
    left(e_send.at[0:240], 1)
    left(u_near.at[0:240], 2)
    left(m_one.at[0:15], 3)
    left(e_turn.at[0:7], 4)
    left(u_batch.at[0:3], 5)
    left(e_own.at[0:3], 7)
    left(m_two.at[0:7], 8)
    left(g_send.at[0:240], 6)
    left(g_turn.at[0:7], 9)
    left(m_three.at[0:3], 10)

def grid_kernel(
    v_grid, v_mix, ix, iz, v_spectral, v_mixgrad, out_hbm, spectral_hbm, mixgrad_hbm, v_out, sems
):
    copies = [
        pltpu.make_async_copy(v_spectral, spectral_hbm, sems.at[4]),
        pltpu.make_async_copy(v_mixgrad, mixgrad_hbm, sems.at[5]),
    ]
    for copy in copies:
        copy.start()
    stacked = []
    for g in range(4):
        received = v_grid[:, 32 * g : 32 * g + 32].reshape(8, 4, 8, 32)
        spectra = lanes([received[:, n].reshape(64, 32) for n in range(4)])
        high, low = halves(spectra)
        along_x = dot(ix[...], jnp.concatenate([high, low, high], axis=0))
        stacked.append(lanes([along_x[:N], along_x[N:]]).astype(BF16))
    stacked = jnp.concatenate(stacked, axis=0)
    for n in range(4):
        grid = dot(stacked, iz[:, 256 * n : 256 * n + 256])
        for g in range(4):
            for r in range(2):
                i = 8 * g + 2 * n + r
                block = grid[N * g : N * g + N, N * r : N * r + N]
                v_out[g, 2 * n + r] = (block + v_mix[i]).astype(BF16)
        copy = pltpu.make_async_copy(
            v_out.at[:, 2 * n : 2 * n + 2], out_hbm.at[:, 2 * n : 2 * n + 2], sems.at[n]
        )
        copy.start()
        copies.append(copy)
    for copy in copies:
        copy.wait()


def on_device(inputs, pre_act, cotangent, spectral_weight, skip_weight):
    field = (CHANNELS, N, N)
    tables = [jnp.asarray(v) for v in make_tables()]
    exchange = [
        pltpu.VMEM((256, N), F32), pltpu.VMEM((256, N), F32),
        pltpu.VMEM((8, 32, N), F32), pltpu.VMEM((256, N), F32),
    ]
    anywhere = pl.BlockSpec(memory_space=pl.ANY)
    near = pl.BlockSpec(memory_space=pltpu.VMEM)
    spectral_type = jax.ShapeDtypeStruct((2, CHANNELS, 8, N), F32)
    skip_type = jax.ShapeDtypeStruct((CHANNELS, CHANNELS), F32)
    operands = [
        inputs.reshape(field), pre_act.reshape(field), cotangent.reshape(field),
        spectral_weight, skip_weight, *tables,
    ]
    stages = pl.pallas_call(
        spectral_kernel,
        out_shape=(
            jax.ShapeDtypeStruct((256, N), F32),
            jax.ShapeDtypeStruct(field, F32),
            jax.ShapeDtypeStruct(tables[4].shape, BF16),
            jax.ShapeDtypeStruct(tables[5].shape, BF16),
            spectral_type,
            skip_type,
        ),
        in_specs=[anywhere] * 11,
        out_specs=(near,) * 6,
        scratch_shapes=[
            pltpu.VMEM(field, BF16), pltpu.VMEM(field, BF16), pltpu.VMEM(field, BF16),
            pltpu.VMEM((2, 32, 32, N), BF16), pltpu.VMEM((32, 32), BF16),
            *(pltpu.VMEM(v.shape, BF16) for v in tables[:4]),
            pltpu.VMEM(field, BF16),
            *exchange, pltpu.VMEM((256, N), F32), pltpu.VMEM((256, N), F32), *exchange,
            *exchange,
            pltpu.VMEM((64, N), F32), pltpu.VMEM((BATCH, 64, N), F32),
            pltpu.VMEM((4, 16, N), F32), pltpu.VMEM((BATCH, 16, N), F32),
            pltpu.VMEM((2, N, N), F32), pltpu.VMEM((2, 256, N), F32), pltpu.VMEM((2, N, N), F32),
            pltpu.VMEM((512, 512), F32), pltpu.VMEM((4, 256, N), F32),
            pltpu.VMEM((512, 512), BF16), pltpu.VMEM((4, 32, N), F32),
            pltpu.VMEM((8, N), F32), pltpu.VMEM((16, 8, N), F32),
            pltpu.VMEM((8, N), F32), pltpu.VMEM((8, 8, N), F32),
            pltpu.VMEM((8, N), F32), pltpu.VMEM((BATCH, 8, N), F32),
            pltpu.SemaphoreType.DMA((17,)),
            pltpu.SemaphoreType.DMA((11,)), pltpu.SemaphoreType.DMA((11,)),
        ],
        compiler_params=pltpu.CompilerParams(
            collective_id=0, has_side_effects=True, vmem_limit_bytes=40 * 2**20
        ),
    )(*(pltpu.with_memory_space_constraint(v, pltpu.HBM) for v in operands))
    grad_inputs, grad_spectral, grad_skip = pl.pallas_call(
        grid_kernel,
        out_shape=(jax.ShapeDtypeStruct((4, 8, N, N), BF16), spectral_type, skip_type),
        in_specs=[near] * 6,
        out_specs=(anywhere,) * 3,
        scratch_shapes=[pltpu.VMEM((4, 8, N, N), BF16), pltpu.SemaphoreType.DMA((6,))],
        compiler_params=pltpu.CompilerParams(vmem_limit_bytes=24 * 2**20),
    )(*stages)
    return grad_inputs.reshape(inputs.shape), grad_spectral, grad_skip


def solution(mesh):
    placed = (
        P("batch", None, None, "space", None),
        P("batch", None, None, "space", None),
        P("batch", None, None, "space", None),
        P(None, None, None, "space"),
        P(),
    )
    return jax.shard_map(
        on_device,
        mesh=mesh,
        in_specs=placed,
        out_specs=(P("batch", None, None, "space", None), P(None, None, "batch", "space"), P()),
        check_vma=False,
    )
```

```python
import math

import jax
import jax.numpy as jnp
import ml_dtypes
import numpy as np
from jax import lax
from jax.experimental import pallas as pl
from jax.experimental.pallas import tpu as pltpu
from jax.sharding import PartitionSpec as P

N = 128
MODES = 32
BATCH = 4
CHANNELS = 32
F32 = jnp.float32
BF16 = jnp.bfloat16
MESH = pl.DeviceIdType.MESH


def signed(index):
    return np.where(index < 16, index, index - 32)


def phases(points, orders):
    angles = np.mod(points[:, None] * orders[None, :], N) * (2.0 * math.pi / N)
    return np.cos(angles), np.sin(angles)


def bf16(table):
    return table.astype(np.float32).astype(ml_dtypes.bfloat16)


def split(table):
    high = bf16(table)
    return high, bf16(table - high.astype(np.float64))


def places():
    t = np.arange(16)
    return t // 4, t // 2 % 2, t % 2


def make_tables():
    points = np.arange(N)
    eye = np.eye(8)
    cos_z, sin_z = (v.reshape(N, 4, 4) for v in phases(points, np.arange(16)))
    fwd_z = np.stack([np.einsum("zqk,cd->czqdk", v, eye) for v in (cos_z, -sin_z)], axis=2)
    fwd_z = fwd_z.reshape(8 * N, 256)
    inv_z = np.stack([np.einsum("zqk,cd->qckdz", v, eye) for v in (cos_z, -sin_z)], axis=0)
    inv_z = inv_z.reshape(256, 8 * N)
    cos_x, sin_x = phases(points, signed(np.arange(32)))
    cos_x, sin_x = bf16(cos_x).astype(np.float64), bf16(sin_x).astype(np.float64)
    parts = np.stack([np.stack([cos_x, sin_x]), np.stack([-sin_x, cos_x])])
    parts = parts.reshape(2, 2, N, 2, 8, 2)
    fwd_x = np.transpose(parts, (3, 5, 0, 4, 1, 2)).reshape(64, 256)
    cos_x, sin_x = phases(points, signed(np.arange(32)))
    parts = np.stack([np.stack([cos_x, -sin_x]), np.stack([sin_x, cos_x])]).reshape(2, 2, N, 2, 8, 2)
    inv_x = np.transpose(parts, (0, 2, 4, 3, 5, 1)).reshape(256, 64)
    q, a, h = places()
    y = a[None, :] * 64 + np.arange(8)[:, None] * 8 + h[None, :] * 4 + q[None, :]
    cos_y, sin_y = phases(y.reshape(-1), signed(np.arange(32)))
    cos_y, sin_y = cos_y.reshape(8, 16, 32), sin_y.reshape(8, 16, 32)
    parts = np.stack([np.stack([cos_y, sin_y]), np.stack([-sin_y, cos_y])])
    fwd_y = np.transpose(parts, (2, 3, 1, 0, 4))[:, :, :, :, None, :]
    fwd_y = np.broadcast_to(fwd_y, (8, 16, 2, 2, 4, 32)).reshape(256, 256)
    parts = np.stack([np.stack([cos_y, -sin_y]), np.stack([sin_y, cos_y])])
    inv_y = np.transpose(parts, (3, 0, 2, 1, 4))[:, :, :, :, None, :]
    inv_y = np.broadcast_to(inv_y, (16, 2, 8, 2, 4, 32)).reshape(256, 256)
    inv_x_high, inv_x_low = split(inv_x)
    inv_x = np.concatenate([inv_x_high, inv_x_high, inv_x_low], axis=1)
    fwd_y, inv_y = np.stack(split(fwd_y)), np.stack(split(inv_y))
    return bf16(fwd_z), bf16(fwd_x), fwd_y, inv_y, inv_x, bf16(inv_z)


def gelu_slope(values):
    normal_cdf = 0.5 * (1.0 + lax.erf(values * (1.0 / math.sqrt(2.0))))
    density = jnp.exp(-0.5 * values * values) * (1.0 / math.sqrt(2.0 * math.pi))
    return normal_cdf + values * density


def dot(left, right):
    return jnp.dot(left, right, preferred_element_type=F32)


def halves(value):
    high = value.astype(BF16)
    return high, (value - high.astype(F32)).astype(BF16)


def product(left, right, contracted):
    first = jnp.concatenate([left[0], left[1], left[0]], axis=contracted[0])
    second = jnp.concatenate([right[0], right[0], right[1]], axis=contracted[1])
    return lax.dot_general(
        first, second, ((contracted[:1], contracted[1:]), ((), ())), preferred_element_type=F32
    )


def lanes(blocks):
    return jnp.concatenate(blocks, axis=1)


def all_sections(field, table_z, table_x):
    planes = [
        jnp.concatenate([field[8 * g + j] for g in range(4)], axis=0) for j in range(8)
    ]
    along_z = dot(lanes(planes), table_z[...])
    both = jnp.concatenate(
        [
            lanes([along_z[N * g : N * g + N, N * part : N * part + N] for g in range(4)])
            for part in range(2)
        ],
        axis=0,
    ).astype(BF16)
    found = dot(table_x[...], both)
    return [found[:, N * g : N * g + N] for g in range(4)]


def to_blocks(sections, sent):
    for q in range(4):
        sent[64 * q : 64 * q + 64, :] = lanes([v[:, 32 * q : 32 * q + 32] for v in sections])


def turn(received, sent):
    for b in range(8):
        sent[b] = received[pl.ds(b, 32, stride=8), :]


def cross(received, sent):
    for t in range(16):
        for part in range(2):
            sent[16 * t + 8 * part : 16 * t + 8 * part + 8, :] = received[
                pl.ds(2 * t + part, 8, stride=32), :
            ]


def k4_lanes(rows):
    return lax.broadcasted_iota(jnp.int32, (rows, N), 1) // 32


def along_y(received, table_y, rows, put):
    both = product(
        halves(received[...]), (table_y[0], table_y[1]), (0, 0)
    )
    block = k4_lanes(32)
    for part in range(2):
        rows[part] = both[:, N * part : N * part + N]
        value = rows[part, pl.ds(0, 32, stride=4), :]
        for k4 in range(1, 4):
            value = jnp.where(block == k4, rows[part, pl.ds(k4, 32, stride=4), :], value)
        put(part, value)


def spectral_kernel(
    in_hbm, pre_hbm, cot_hbm, weight_hbm, skip_hbm,
    fz_hbm, fx_hbm, fy_hbm, iy_hbm, ix_hbm, iz_hbm,
    v_grid, v_mix, ix, iz, v_spectral, v_mixgrad,
    v_in, v_pre, v_cot, v_weight, v_skip, fz, fx, fy, iy,
    v_cp,
    u_send, u_mid, u_turn, u_all, u_near, u_last, e_send, e_mid, e_turn, e_all, g_send, g_mid, g_turn, g_all,
    u_own, u_batch, e_own, e_batch, rows, partial, back_rows,
    prod, prod_rows, kron, skip_rows, m_own, m_one, m_two_own, m_two, m_three_own, m_three,
    load_sem, send_sem, recv_sem,
):
    pairs = [
        (pre_hbm, v_pre), (cot_hbm, v_cot), (fz_hbm, fz), (fx_hbm, fx), (in_hbm, v_in),
        (skip_hbm, v_skip), (fy_hbm, fy), (weight_hbm, v_weight), (iy_hbm, iy), (ix_hbm, ix),
        (iz_hbm, iz),
    ]
    loads = [
        pltpu.make_async_copy(src, dst, load_sem.at[n]) for n, (src, dst) in enumerate(pairs)
    ]
    for copy in loads[:4]:
        copy.start()

    sample = lax.axis_index("batch")
    place = lax.axis_index("space")
    a = place // 64
    b = place // 8 % 8
    h = place // 4 % 2
    q = place % 4
    t = 4 * q + 2 * a + h

    def near(k):
        peer = (t + k) % 16
        return peer, peer // 2 % 2 * 64 + b * 8 + peer % 2 * 4 + peer // 4

    def near_first():
        z = place % 8
        for step in (4, 3, 5, 2, 6, 1, 7, 0):
            c = (z + step) % 8
            for side in (1 - a, a):
                if step or side is not a:
                    yield c % 4 * 4 + side * 2 + c // 4, side * 64 + b * 8 + c

    def far(k):
        peer = (b + k) % 8
        return peer, a * 64 + peer * 8 + h * 4 + q

    def far_first():
        return [far(k) for k in (4, 3, 5, 2, 6, 1, 7)]

    def other(k):
        return (sample + k) % BATCH

    barrier = pltpu.get_barrier_semaphore()
    near_places, far_places = list(near_first()), far_first()
    by_distance = near_places[:2] + far_places[:1] + near_places[2:6] + far_places[1:3]
    for _, where in by_distance + near_places[6:] + far_places[3:]:
        pl.semaphore_signal(barrier, inc=1, device_id={"space": where}, device_id_type=MESH)

    @pl.loop(1, BATCH)
    def _(k):
        pl.semaphore_signal(barrier, inc=1, device_id={"batch": other(k)}, device_id_type=MESH)

    def remote(src, dst, n, where):
        return pltpu.make_async_remote_copy(
            src_ref=src, dst_ref=dst, send_sem=send_sem.at[n], recv_sem=recv_sem.at[n],
            device_id=where, device_id_type=MESH,
        )

    def rows16(ref, slot):
        return ref.at[pl.ds(pl.multiple_of(slot * 16, 16), 16), :]

    def send_near(src, dst, n):
        for peer, where in near_first():
            remote(rows16(src, peer), rows16(dst, t), n, {"space": where}).start()
        pltpu.make_async_copy(rows16(src, t), rows16(dst, t), recv_sem.at[n]).start()

    def send_far(src, dst, n):
        mine = dst.at[pl.ds(pl.multiple_of(b * 32, 32), 32), :]
        for peer, where in far_first():
            remote(src.at[peer], mine, n, {"space": where}).start()
        pltpu.make_async_copy(src.at[b], mine, recv_sem.at[n]).start()

    def send_batch(src, dst, n):
        pltpu.make_async_copy(src, dst.at[sample], recv_sem.at[n]).start()

        @pl.loop(1, BATCH)
        def _(k):
            remote(src, dst.at[sample], n, {"batch": other(k)}).start()

    def arrived(ref, n):
        pltpu.make_async_copy(ref, ref, recv_sem.at[n]).wait()

    def left(ref, n):
        pltpu.make_async_copy(ref, ref, send_sem.at[n]).wait()

    loads[4].start()
    loads[0].wait()
    loads[1].wait()
    for g in range(4):
        for c in range(8 * g, 8 * g + 8):
            slope = gelu_slope(v_pre[c].astype(F32))
            v_cp[c] = (v_cot[c].astype(F32) * slope).astype(BF16)
    loads[2].wait()
    loads[3].wait()
    sections = all_sections(v_cp, fz, fx)
    to_blocks(sections, e_send)
    pl.semaphore_wait(barrier, 15 + 7 + BATCH - 1)
    send_near(e_send, e_mid, 1)
    for copy in loads[5:]:
        copy.start()

    loads[4].wait()
    to_blocks(all_sections(v_in, fz, fx), u_send)
    turn(u_send, u_turn)
    send_far(u_turn, u_mid, 0)

    chunks = range(8)
    prod[...] = lax.dot_general(
        lanes([v_in[:, 16 * j : 16 * j + 16, :].reshape(512, N) for j in chunks]),
        lanes([v_cp[:, 16 * j : 16 * j + 16, :].reshape(512, N) for j in chunks]),
        (((1,), (1,)), ((), ())),
        preferred_element_type=F32,
    )
    row16 = lax.broadcasted_iota(jnp.int32, (16, 512), 0)
    column = lax.broadcasted_iota(jnp.int32, (16, 512), 1)
    same = row16 == column % 16
    for i in range(CHANNELS):
        kept = jnp.where(same, prod[16 * i : 16 * i + 16, :], 0.0)
        kept = kept[:8] + kept[8:]
        for n in range(4):
            prod_rows[n, 8 * i : 8 * i + 8, :] = kept[:, N * n : N * n + N]
    summed = []
    for n in range(4):
        value = prod_rows[n, pl.ds(0, 32, stride=8), :]
        for j in range(1, 8):
            value = value + prod_rows[n, pl.ds(j, 32, stride=8), :]
        summed.append(value)
    summed = lanes(summed)
    wide = lax.broadcasted_iota(jnp.int32, (512, 32), 0) // 16
    spread = wide == lax.broadcasted_iota(jnp.int32, (512, 32), 1)
    own = jnp.dot(
        summed, spread.astype(F32), precision=lax.Precision.HIGHEST, preferred_element_type=F32
    )
    m_own[...] = lanes([own[8 * r : 8 * r + 8, :] for r in range(4)])

    pltpu.make_async_copy(m_own, m_one.at[t], recv_sem.at[3]).start()

    @pl.loop(1, 16)
    def _(k):
        remote(m_own, m_one.at[t], 3, {"space": near(k)[1]}).start()

    arrived(e_mid, 1)
    turn(e_mid, e_turn)
    send_far(e_turn, e_all, 4)
    arrived(u_mid, 0)
    cross(u_mid, u_near)
    send_near(u_near, u_last, 2)

    loads[5].wait()
    tall = lax.broadcasted_iota(jnp.int32, (32, 512), 1) // 16
    spread_t = tall == lax.broadcasted_iota(jnp.int32, (32, 512), 0)
    repeated = dot(v_skip[...], spread_t.astype(F32).astype(BF16))
    for n in range(4):
        skip_rows[n] = repeated[:, N * n : N * n + N]
    for i in range(CHANNELS):
        row = lanes([skip_rows[n, pl.ds(i, 16, stride=0), :] for n in range(4)])
        kron[16 * i : 16 * i + 16, :] = jnp.where(same, row, 0.0).astype(BF16)
    for j in range(0, 8, 2):
        pair = [v_cp[:, 16 * n : 16 * n + 16, :].reshape(512, N) for n in (j, j + 1)]
        mixed = dot(kron[...], lanes(pair))
        for n in range(2):
            v_mix[:, 16 * (j + n) : 16 * (j + n) + 16, :] = mixed[:, N * n : N * n + N].reshape(
                32, 16, N
            )

    arrived(m_one, 3)
    total = m_one[0]
    for n in range(1, 16):
        total = total + m_one[n]
    m_two_own[...] = total
    pltpu.make_async_copy(m_two_own, m_two.at[b], recv_sem.at[8]).start()

    @pl.loop(1, 8)
    def _(k):
        remote(m_two_own, m_two.at[b], 8, {"space": far(k)[1]}).start()

    arrived(e_all, 4)
    loads[6].wait()
    e_rounded = []

    def put_e(part, value):
        for block in range(4):
            e_own[block, 8 * part : 8 * part + 8, :] = value[8 * block : 8 * block + 8, :]
        e_rounded.append(value.astype(BF16).astype(F32))

    along_y(e_all, fy, rows, put_e)

    loads[7].wait()
    e_real, e_imag = e_rounded
    for i in range(CHANNELS):
        w_real = v_weight[0, i].astype(F32)
        w_imag = v_weight[1, i].astype(F32)
        real = w_real * e_real + w_imag * e_imag
        imag = w_real * e_imag - w_imag * e_real
        for part, value in enumerate((real, imag)):
            partial[part, 8 * i : 8 * i + 8, :] = (
                value[0:8] + value[8:16] + (value[16:24] + value[24:32])
            )
    lane = lax.broadcasted_iota(jnp.int32, (1, N), 1)
    zero_kz = jnp.logical_and(q == 0, lane < 32)
    scale = jnp.where(zero_kz, 1.0, 2.0).astype(F32) / float(N * N * N)
    block = k4_lanes(32)
    for part in range(2):
        value = partial[part, pl.ds(0, 32, stride=8), :]
        for j in range(1, 8):
            value = value + partial[part, pl.ds(j, 32, stride=8), :]
        value = value * scale
        for k4 in range(4):
            back_rows[part, pl.ds(k4, 32, stride=4), :] = jnp.where(block == k4, value, 0.0)
    loads[8].wait()
    back = halves(lanes([back_rows[0], back_rows[1]]))
    g_send[...] = product((iy[0], iy[1]), back, (1, 1))
    send_near(g_send, g_mid, 6)

    pltpu.make_async_copy(e_own.at[sample], e_batch.at[sample], recv_sem.at[7]).start()

    @pl.loop(1, BATCH)
    def _(k):
        peer = other(k)
        remote(e_own.at[peer], e_batch.at[sample], 7, {"batch": peer}).start()

    arrived(u_last, 2)
    for n in range(8):
        u_all[32 * n : 32 * n + 32, :] = u_last[pl.ds(n, 32, stride=8), :]

    def put_u(part, value):
        u_own[32 * part : 32 * part + 32, :] = value

    along_y(u_all, fy, rows, put_u)
    send_batch(u_own, u_batch, 5)

    arrived(m_two, 8)
    total = m_two[0]
    for n in range(1, 8):
        total = total + m_two[n]
    m_three_own[...] = total
    send_batch(m_three_own, m_three, 10)

    arrived(g_mid, 6)
    turn(g_mid, g_turn)
    send_far(g_turn, g_all, 9)

    arrived(u_batch, 5)
    arrived(e_batch, 7)
    for i in range(CHANNELS):
        real = jnp.zeros((8, N), F32)
        imag = jnp.zeros((8, N), F32)
        for n in range(BATCH):
            u_real = u_batch[n, pl.ds(i, 8, stride=0), :]
            u_imag = u_batch[n, pl.ds(32 + i, 8, stride=0), :]
            e_r = e_batch[n, 0:8, :]
            e_i = e_batch[n, 8:16, :]
            real = real + (u_real * e_r + u_imag * e_i)
            imag = imag + (u_real * e_i - u_imag * e_r)
        v_spectral[0, i] = real * scale
        v_spectral[1, i] = imag * scale

    arrived(m_three, 10)
    total = (m_three[0] + m_three[1] + (m_three[2] + m_three[3])) / math.sqrt(BATCH * N * N * N)
    for r in range(4):
        v_mixgrad[8 * r : 8 * r + 8, :] = total[:, 32 * r : 32 * r + 32]

    loads[9].wait()
    loads[10].wait()
    arrived(g_all, 9)
    v_grid[...] = g_all[...]

    left(u_turn.at[0:7], 0)
    left(e_send.at[0:240], 1)
    left(u_near.at[0:240], 2)
    left(m_one.at[0:15], 3)
    left(e_turn.at[0:7], 4)
    left(u_batch.at[0:3], 5)
    left(e_own.at[0:3], 7)
    left(m_two.at[0:7], 8)
    left(g_send.at[0:240], 6)
    left(g_turn.at[0:7], 9)
    left(m_three.at[0:3], 10)

def grid_kernel(
    v_grid, v_mix, ix, iz, v_spectral, v_mixgrad, out_hbm, spectral_hbm, mixgrad_hbm, v_out, sems
):
    copies = [
        pltpu.make_async_copy(v_spectral, spectral_hbm, sems.at[4]),
        pltpu.make_async_copy(v_mixgrad, mixgrad_hbm, sems.at[5]),
    ]
    for copy in copies:
        copy.start()
    stacked = []
    for g in range(4):
        received = v_grid[:, 32 * g : 32 * g + 32].reshape(8, 4, 8, 32)
        spectra = lanes([received[:, n].reshape(64, 32) for n in range(4)])
        high, low = halves(spectra)
        along_x = dot(ix[...], jnp.concatenate([high, low, high], axis=0))
        stacked.append(lanes([along_x[:N], along_x[N:]]).astype(BF16))
    stacked = jnp.concatenate(stacked, axis=0)
    for n in range(4):
        grid = dot(stacked, iz[:, 256 * n : 256 * n + 256])
        for g in range(4):
            for r in range(2):
                i = 8 * g + 2 * n + r
                block = grid[N * g : N * g + N, N * r : N * r + N]
                v_out[g, 2 * n + r] = (block + v_mix[i]).astype(BF16)
        copy = pltpu.make_async_copy(
            v_out.at[:, 2 * n : 2 * n + 2], out_hbm.at[:, 2 * n : 2 * n + 2], sems.at[n]
        )
        copy.start()
        copies.append(copy)
    for copy in copies:
        copy.wait()


def on_device(inputs, pre_act, cotangent, spectral_weight, skip_weight):
    field = (CHANNELS, N, N)
    tables = [jnp.asarray(v) for v in make_tables()]
    exchange = [
        pltpu.VMEM((256, N), F32), pltpu.VMEM((256, N), F32),
        pltpu.VMEM((8, 32, N), F32), pltpu.VMEM((256, N), F32),
    ]
    anywhere = pl.BlockSpec(memory_space=pl.ANY)
    near = pl.BlockSpec(memory_space=pltpu.VMEM)
    spectral_type = jax.ShapeDtypeStruct((2, CHANNELS, 8, N), F32)
    skip_type = jax.ShapeDtypeStruct((CHANNELS, CHANNELS), F32)
    operands = [
        inputs.reshape(field), pre_act.reshape(field), cotangent.reshape(field),
        spectral_weight, skip_weight, *tables,
    ]
    stages = pl.pallas_call(
        spectral_kernel,
        out_shape=(
            jax.ShapeDtypeStruct((256, N), F32),
            jax.ShapeDtypeStruct(field, F32),
            jax.ShapeDtypeStruct(tables[4].shape, BF16),
            jax.ShapeDtypeStruct(tables[5].shape, BF16),
            spectral_type,
            skip_type,
        ),
        in_specs=[anywhere] * 11,
        out_specs=(near,) * 6,
        scratch_shapes=[
            pltpu.VMEM(field, BF16), pltpu.VMEM(field, BF16), pltpu.VMEM(field, BF16),
            pltpu.VMEM((2, 32, 32, N), BF16), pltpu.VMEM((32, 32), BF16),
            *(pltpu.VMEM(v.shape, BF16) for v in tables[:4]),
            pltpu.VMEM(field, BF16),
            *exchange, pltpu.VMEM((256, N), F32), pltpu.VMEM((256, N), F32), *exchange,
            *exchange,
            pltpu.VMEM((64, N), F32), pltpu.VMEM((BATCH, 64, N), F32),
            pltpu.VMEM((4, 16, N), F32), pltpu.VMEM((BATCH, 16, N), F32),
            pltpu.VMEM((2, N, N), F32), pltpu.VMEM((2, 256, N), F32), pltpu.VMEM((2, N, N), F32),
            pltpu.VMEM((512, 512), F32), pltpu.VMEM((4, 256, N), F32),
            pltpu.VMEM((512, 512), BF16), pltpu.VMEM((4, 32, N), F32),
            pltpu.VMEM((8, N), F32), pltpu.VMEM((16, 8, N), F32),
            pltpu.VMEM((8, N), F32), pltpu.VMEM((8, 8, N), F32),
            pltpu.VMEM((8, N), F32), pltpu.VMEM((BATCH, 8, N), F32),
            pltpu.SemaphoreType.DMA((11,)),
            pltpu.SemaphoreType.DMA((11,)), pltpu.SemaphoreType.DMA((11,)),
        ],
        compiler_params=pltpu.CompilerParams(
            collective_id=0, has_side_effects=True, vmem_limit_bytes=40 * 2**20
        ),
    )(*(pltpu.with_memory_space_constraint(v, pltpu.HBM) for v in operands))
    grad_inputs, grad_spectral, grad_skip = pl.pallas_call(
        grid_kernel,
        out_shape=(jax.ShapeDtypeStruct((4, 8, N, N), BF16), spectral_type, skip_type),
        in_specs=[near] * 6,
        out_specs=(anywhere,) * 3,
        scratch_shapes=[pltpu.VMEM((4, 8, N, N), BF16), pltpu.SemaphoreType.DMA((6,))],
        compiler_params=pltpu.CompilerParams(vmem_limit_bytes=24 * 2**20),
    )(*stages)
    return grad_inputs.reshape(inputs.shape), grad_spectral, grad_skip


def solution(mesh):
    placed = (
        P("batch", None, None, "space", None),
        P("batch", None, None, "space", None),
        P("batch", None, None, "space", None),
        P(None, None, None, "space"),
        P(),
    )
    return jax.shard_map(
        on_device,
        mesh=mesh,
        in_specs=placed,
        out_specs=(P("batch", None, None, "space", None), P(None, None, "batch", "space"), P()),
        check_vma=False,
    )
```
